256 devices in a mesh: scen: 16 (over z, core), inst: 16 (over x, y).
Axes of the slice: x: 4, y: 4, z: 8, core: 2. Of those that a mesh axis runs over, the one named last changes fastest.
Arguments:
- shocks: bfloat16 [8192, 2048], P('scen', 'inst'), may hold values from -6 to 6
- loadings: bfloat16 [2048, 65536], P(None, 'inst'), may hold values from -0.125 to 0.125
- delta: float32 [65536], P('inst'), may hold values from -6 to 6
- gamma: float32 [65536], P('inst'), may hold values from -3 to 3
- kappa: float32 [65536], P('inst'), may hold values from -1.2 to 1.2
- book_of: int32 [65536], P('inst'), may hold values from 0 to 255
- bracket_low: int32 [256], replicated, may hold values from -48 to -25
- bracket_high: int32 [256], replicated, may hold values from -24 to 8
- rank: int32 [256], replicated, may hold values from 64 to 128
Outputs:
- contribution: float32 [256, 65536], P('scen', 'inst')
- quantile: float32 [256], P('inst')
The draws below stay inside these ranges and needn't reach their ends.
Inputs may be any that keep to these rules, and one draw needn't show every extreme that they name: `book_of`: each instrument's book.
All inputs are finite; a program needn't handle non-finite values.
Results may differ from the reference program's by a relative error of at most 0.002.
Values may be sent and summed in bfloat16 or wider, within the bound.
A program may use at most 128 MiB of HBM per device.

```python
import jax
import jax.numpy as jnp
from jax import lax

FACTORS = 2048
BOOKS = 256
PIVOTS = 64
ROUNDS = 3
INST_DEV = 4096
SCEN = 8192
INST = 65536
N_INST = 16


def set_ends(array, own_key, smallest, high):
    longest = array.shape.index(max(array.shape))
    spots = []
    for shift in (0, 1):
        where = [jax.random.randint(jax.random.fold_in(own_key, axis), (), 0, length) for axis, length in enumerate(array.shape)]
        where[longest] = (where[longest] + shift) % array.shape[longest]
        spots.append(tuple(where))
    return array.at[spots[0]].set(smallest).at[spots[1]].set(high)


def block_levels(key, extent, shards, low, top_value):
    level, own = 1.0, jax.random.fold_in(key, 6)
    for axis_at, parts in shards:
        heights = jnp.exp(jax.random.uniform(jax.random.fold_in(own, axis_at), (parts,), jnp.float32, low / len(shards), top_value / len(shards)))
        level = level * jnp.repeat(heights, extent[axis_at] // parts).reshape([-1 if axis == axis_at else 1 for axis in range(len(extent))])
    return level


def noise(own_key, dims, scale, bound, split=(), held_as=jnp.bfloat16):
    factor_of = block_levels(own_key, dims, split, -0.22, 0.18) if split else 1.0
    array = jax.random.normal(own_key, dims, jnp.float32) * scale * factor_of
    return jnp.minimum(jnp.maximum(array, -bound), bound).astype(held_as)


def setup_inputs(seed: int = 0) -> dict:
    seeds = jax.random.split(jax.random.key(seed), 10)
    return {
        "shocks": noise(seeds[0], (SCEN, FACTORS), 1.0, 6.0, ((0, 16), (1, 16))),
        "loadings": noise(seeds[1], (FACTORS, INST), FACTORS ** -0.5, 0.125, ((1, 16),)),
        "delta": noise(seeds[2], (INST,), 1.0, 6.0, ((0, 16),), jnp.float32),
        "gamma": noise(seeds[3], (INST,), 0.5, 3.0, ((0, 16),), jnp.float32),
        "kappa": noise(seeds[4], (INST,), 0.2, 1.2, ((0, 16),), jnp.float32),
        "book_of": set_ends(jax.random.randint(seeds[5], (INST,), 0, BOOKS), jax.random.fold_in(seeds[5], 1), 0, BOOKS - 1).astype(jnp.int32),
        "bracket_low": set_ends(jax.random.randint(seeds[6], (BOOKS,), -48, -24), jax.random.fold_in(seeds[6], 1), -48, (-24) - 1).astype(jnp.int32),
        "bracket_high": set_ends(jax.random.randint(seeds[7], (BOOKS,), -24, 9), jax.random.fold_in(seeds[7], 1), -24, 8).astype(jnp.int32),
        "rank": set_ends(jax.random.randint(seeds[8], (BOOKS,), SCEN // 128, SCEN // 64 + 1), jax.random.fold_in(seeds[8], 1), SCEN // 128, (SCEN // 64 + 1) - 1).astype(jnp.int32),
    }


tail_width = 0.5
bracket_unit = 0.125


def revalue(moves, delta, gamma, kappa):
    return (moves * (delta + moves * (gamma + moves * kappa))).astype(jnp.bfloat16)


def count_below(book_pnl, pivots):
    group = min(book_pnl.shape[1], 32)
    blocks = book_pnl.T.reshape(-1, group, book_pnl.shape[0])
    pivot_blocks = pivots.reshape(-1, group, pivots.shape[1])

    def one_block(pair):
        values, marks = pair
        return jnp.sum((values[:, :, None] <= marks[:, None, :]).astype(jnp.int32), axis=1)

    return lax.map(one_block, (blocks, pivot_blocks)).reshape(pivots.shape)


def locate(book_pnl, bracket_low, bracket_high, rank, total):
    lower = bracket_low.astype(jnp.float32) * bracket_unit
    upper = bracket_high.astype(jnp.float32) * bracket_unit
    marks = jnp.arange(PIVOTS, dtype=jnp.int32)
    levels = marks.astype(jnp.float32)
    for sweep_index in range(ROUNDS):
        spacing = (upper - lower) / (PIVOTS - 1)
        pivots = lower[:, None] + levels[None, :] * spacing[:, None]
        counts = total(count_below(book_pnl, pivots))
        below = jnp.sum((counts < rank[:, None]).astype(jnp.int32), axis=1)
        chosen = jnp.clip(below, 1, PIVOTS - 1)
        lower = jnp.sum(jnp.where(marks[None, :] == (chosen - 1)[:, None], pivots, 0.0), axis=1)
        upper = jnp.sum(jnp.where(marks[None, :] == chosen[:, None], pivots, 0.0), axis=1)
    return (lower + upper) * 0.5


def reference(shocks, loadings, delta, gamma, kappa, book_of, bracket_low, bracket_high, rank):
    width = INST_DEV
    blocks = N_INST
    scale = (BOOKS / (width * blocks)) ** 0.5
    load_blocks = loadings.reshape(FACTORS, blocks, width).transpose(1, 0, 2)
    books = jnp.arange(BOOKS, dtype=jnp.int32)

    def one_block(pieces):
        load_part, delta_part, gamma_part, kappa_part, book_part = pieces
        moves = jnp.dot(shocks, load_part, preferred_element_type=jnp.float32)
        profit = revalue(moves, delta_part, gamma_part, kappa_part)
        onehot = (book_part[:, None] == books[None, :]).astype(jnp.bfloat16)
        return profit, jnp.dot(profit, onehot, preferred_element_type=jnp.float32) * scale

    profit_blocks, partials = lax.map(one_block, (load_blocks, delta.reshape(blocks, width), gamma.reshape(blocks, width), kappa.reshape(blocks, width), book_of.reshape(blocks, width)))
    book_pnl = jnp.sum(partials, axis=0)
    quantile = locate(book_pnl, bracket_low, bracket_high, rank, lambda counts: counts)
    weights = jax.nn.sigmoid((quantile[None, :] - book_pnl) / tail_width).astype(jnp.bfloat16)
    mass = jnp.sum(weights.astype(jnp.float32), axis=0)

    def tail_block(profit):
        return lax.dot_general(weights, profit, (((0,), (0,)), ((), ())), preferred_element_type=jnp.float32)

    terms = lax.map(tail_block, profit_blocks)
    contribution = terms.transpose(1, 0, 2).reshape(BOOKS, blocks * width) / mass[:, None]
    return contribution, quantile
```

```python
import functools

import jax
import jax.numpy as jnp
from jax import lax
from jax.experimental import pallas as pl
from jax.experimental.pallas import tpu as pltpu
from jax.sharding import PartitionSpec as P

MESH = pl.DeviceIdType.MESH
F32 = jnp.float32
BF16 = jnp.bfloat16

PIVOTS = 64
ROUNDS = 3
BOOKS = 256
SIDE = 4
N_INST = 16
N_SCEN = 16
RING = 8
SHARE = 16
SCEN_DEV = 512
HALF = 256
FACT_DEV = 128
FACTORS = 2048
INST_DEV = 4096
TILE = 512
TILES = INST_DEV // TILE
CHUNKS = 4
CHUNK = INST_DEV // CHUNKS
SCALE = (BOOKS / (INST_DEV * N_INST)) ** 0.5


def sigmoid(v):
    return 1.0 / (1.0 + jnp.exp(-v))


def kernel(
    shocks, loadings, delta, gamma, kappa, book_of, low, high, rank,
    out, qout,
    LH, LD, PR, OH, SENS, BK, PS, RS, ROWS, DV, PNL, QR, QA, W,
    SIBS, SIBR, OWNC, RSND, RRCV, OUT,
    ld_sem, in_sem, a_send, a_recv, c_send, c_recv, d_send, d_recv, g_send, g_recv,
    f_send, f_recv, sib_send, sib_recv, r_send, r_recv, o_sem,
):
    s = lax.axis_index("scen")
    i = lax.axis_index("inst")
    x, y = lax.div(i, SIDE), lax.rem(i, SIDE)
    z, c = lax.div(s, 2), lax.rem(s, 2)

    def inst_at(dx, dy):
        return lax.rem(x + dx + SIDE, SIDE) * SIDE + lax.rem(y + dy + SIDE, SIDE)

    def inst_peer(k):
        return lax.rem(i + k, N_INST)

    def scen_peer(k):
        return lax.rem(s + k, N_SCEN)

    def ring_pos(d):
        return lax.rem(z + d + RING, RING)

    def remote(src, dst, ssem, rsem, **dev):
        return pltpu.make_async_remote_copy(
            src_ref=src, dst_ref=dst, send_sem=ssem, recv_sem=rsem,
            device_id=dev, device_id_type=MESH,
        )

    def drain(ref, sem):
        pltpu.make_async_copy(ref, ref, sem).wait()

    own_cols = pl.ds(pl.multiple_of(i * FACT_DEV, FACT_DEV), FACT_DEV)
    small = [
        pltpu.make_async_copy(shocks, LH.at[:, own_cols], in_sem.at[0]),
        pltpu.make_async_copy(delta, SENS.at[0], in_sem.at[1]),
        pltpu.make_async_copy(gamma, SENS.at[1], in_sem.at[2]),
        pltpu.make_async_copy(kappa, SENS.at[2], in_sem.at[3]),
        pltpu.make_async_copy(book_of, BK, in_sem.at[4]),
    ]
    for cp in small:
        cp.start()

    def load_tile(n):
        return pltpu.make_async_copy(
            loadings.at[:, pl.ds(pl.multiple_of(n * TILE, TILE), TILE)], LD.at[n], ld_sem.at[n]
        )

    for n in range(TILES):
        load_tile(n).start()

    barrier = pltpu.get_barrier_semaphore()

    def greet(k, carry):
        pl.semaphore_signal(barrier, inc=1, device_id={"inst": inst_peer(k)}, device_id_type=MESH)
        pl.semaphore_signal(barrier, inc=1, device_id={"scen": scen_peer(k)}, device_id_type=MESH)
        return carry

    lax.fori_loop(1, 16, greet, 0)
    pl.semaphore_wait(barrier, 30)

    def along(colour, first, second):
        return inst_at(first, second) if colour == 0 else inst_at(second, first)

    def rows_of(h, colour, part):
        start = h * HALF + colour * (HALF // 2)
        size = HALF // 2
        if part == 1:
            size //= 2
        elif part == 2:
            size //= 2
            start += size
        return pl.ds(start, size)

    def piece(h, colour, a, b, part):
        k = along(colour, a, b)
        return LH.at[rows_of(h, colour, part), pl.ds(pl.multiple_of(k * FACT_DEV, FACT_DEV), FACT_DEV)]

    def a_pass(h, colour, a, b, part, to_first, to_second, pid):
        there = piece(h, colour, a, b, part)
        src = shocks.at[rows_of(h, colour, part), :] if (a, b) == (0, 0) else there
        remote(
            src, there, a_send, a_recv.at[(h * 2 + colour) * 20 + pid],
            inst=along(colour, to_first, to_second),
        ).start()

    def a_wait(h, colour, a, b, part, pid):
        drain(piece(h, colour, a, b, part), a_recv.at[(h * 2 + colour) * 20 + pid])

    lanes = (0, -1, 1, 2)

    def a_second(h, colour, q):
        a_pass(h, colour, lanes[q], 0, 0, 0, 1, 4 + 4 * q)
        a_pass(h, colour, lanes[q], 0, 0, 0, -1, 5 + 4 * q)

    def a_hand_on(h, colour, q):
        a_wait(h, colour, lanes[q], -1, 0, 4 + 4 * q)
        a_pass(h, colour, lanes[q], -1, 1, 0, 1, 6 + 4 * q)
        a_wait(h, colour, lanes[q], 1, 0, 5 + 4 * q)
        a_pass(h, colour, lanes[q], 1, 2, 0, -1, 7 + 4 * q)

    def a_step(h, step):
        for colour in range(2):
            if step == 0:
                a_pass(h, colour, 0, 0, 0, 1, 0, 0)
                a_pass(h, colour, 0, 0, 0, -1, 0, 1)
                a_second(h, colour, 0)
            elif step == 1:
                a_wait(h, colour, -1, 0, 0, 0)
                a_pass(h, colour, -1, 0, 1, 1, 0, 2)
                a_second(h, colour, 1)
                a_wait(h, colour, 1, 0, 0, 1)
                a_pass(h, colour, 1, 0, 2, -1, 0, 3)
                a_second(h, colour, 2)
            elif step == 2:
                a_hand_on(h, colour, 0)
            elif step == 3:
                a_wait(h, colour, 2, 0, 1, 2)
                a_wait(h, colour, 2, 0, 2, 3)
                a_second(h, colour, 3)
            elif step == 4:
                a_hand_on(h, colour, 1)
                a_hand_on(h, colour, 2)
            elif step == 5:
                a_hand_on(h, colour, 3)
            else:
                for q in range(4):
                    a_wait(h, colour, lanes[q], 2, 1, 6 + 4 * q)
                    a_wait(h, colour, lanes[q], 2, 2, 7 + 4 * q)

    a_step(0, 0)
    small[4].wait()
    book_ids = lax.broadcasted_iota(jnp.int32, (BOOKS, TILE), 0)

    def one_hot(n, carry):
        cols = pl.ds(pl.multiple_of(n * TILE, TILE), TILE)
        OH[:, cols] = jnp.where(BK[:, cols] == book_ids, 1.0, 0.0).astype(BF16)
        return carry

    lax.fori_loop(0, TILES, one_hot, 0)
    for step in range(1, 4):
        a_step(0, step)
    a_step(1, 0)
    a_step(0, 4)
    a_step(0, 5)
    for cp in small[:4]:
        cp.wait()
    a_step(0, 6)

    def share_rows(k):
        return pl.ds(pl.multiple_of(k * SHARE, SHARE), SHARE)

    def send_sums(h):
        def one(k, carry):
            p = inst_peer(k)
            remote(PS.at[h, share_rows(p), :], RS.at[h, i], c_send.at[h], c_recv.at[h], inst=p).start()
            return carry

        lax.fori_loop(1, N_INST, one, 0)
        RS[h, i] = PS[h, share_rows(i), :]

    def take_sums(h):
        drain(RS.at[h, pl.ds(0, N_INST - 1)], c_recv.at[h])
        total = RS[h, 0]
        for k in range(1, N_INST):
            total = total + RS[h, k]
        total = total * SCALE
        PNL[i, h] = total
        for r in range(2):
            ROWS[h, :, r, :] = total[:, r * 128 : (r + 1) * 128]

        def one(k, carry):
            p = scen_peer(k)
            remote(ROWS.at[h, p], DV.at[h, s], d_send.at[h], d_recv.at[h], scen=p).start()
            return carry

        lax.fori_loop(1, N_SCEN, one, 0)

        def other(k, carry):
            p = inst_peer(k)
            remote(PNL.at[i, h], PNL.at[i, h], g_send.at[h], g_recv.at[h], inst=p).start()
            return carry

        lax.fori_loop(1, N_INST, other, 0)
        DV[h, s] = ROWS[h, s]

    def tile(h, n):
        cols = pl.ds(pl.multiple_of(n * TILE, TILE), TILE)
        moves = jnp.dot(LH[pl.ds(h * HALF, HALF), :], LD[n], preferred_element_type=F32)
        d, g, k = SENS[0, :, cols], SENS[1, :, cols], SENS[2, :, cols]
        profit = (moves * (d + moves * (g + moves * k))).astype(BF16)
        PR[pl.ds(h * HALF, HALF), cols] = profit
        part = lax.dot_general(OH[:, cols], profit, (((1,), (1,)), ((), ())), preferred_element_type=F32)
        PS[h] += part

    PS[...] = jnp.zeros_like(PS)

    def first_half(n, carry):
        load_tile(n).wait()
        tile(0, n)
        for step in range(1, 6):
            @pl.when(n == step)
            def _():
                a_step(1, step)
        return carry

    lax.fori_loop(0, TILES, first_half, 0)
    send_sums(0)
    a_step(1, 6)

    def second_half(n, carry):
        tile(1, n)

        @pl.when(n == 5)
        def _():
            take_sums(0)

        return carry

    lax.fori_loop(0, TILES, second_half, 0)
    send_sums(1)
    take_sums(1)

    book = i * SHARE + s
    lower = jnp.full((PIVOTS, 128), low[book], jnp.int32).astype(F32) * 0.125
    upper = jnp.full((PIVOTS, 128), high[book], jnp.int32).astype(F32) * 0.125
    wanted = jnp.full((PIVOTS, 128), rank[book], jnp.int32).astype(F32)
    levels = lax.broadcasted_iota(jnp.int32, (PIVOTS, 128), 0).astype(F32)
    for h in range(2):
        drain(DV.at[h, pl.ds(0, N_SCEN - 1)], d_recv.at[h])
    for _ in range(ROUNDS):
        spacing = (upper - lower) / (PIVOTS - 1)
        marks = lower + levels * spacing
        count = jnp.zeros((PIVOTS, 128), F32)
        for h in range(2):
            for p in range(N_SCEN):
                for r in range(2):
                    row = DV[h, p, pl.ds(r, 1), :]
                    count = count + jnp.where(row <= marks, 1.0, 0.0)
        count = jnp.sum(count, axis=1, keepdims=True)
        below = jnp.sum(jnp.where(count < wanted, 1.0, 0.0), axis=0, keepdims=True)
        chosen = jnp.clip(below, 1.0, PIVOTS - 1.0)
        upper = lower + chosen * spacing
        lower = lower + (chosen - 1.0) * spacing
    quantile = (lower + upper) * 0.5
    pair_q = quantile[0:2, :]
    mass = jnp.zeros((2, 128), F32)
    for h in range(2):
        for p in range(N_SCEN):
            mass = mass + sigmoid((pair_q - DV[h, p]) * 2.0).astype(BF16).astype(F32)
    mass = jnp.sum(jnp.sum(mass, axis=1, keepdims=True), axis=0, keepdims=True)
    lane = lax.broadcasted_iota(jnp.int32, (1, 128), 1)
    QR[s] = jnp.where(lane < 64, quantile[0:1, :], jnp.broadcast_to(mass, (1, 128)))

    def send_q(k, carry):
        remote(QR.at[s], QR.at[s], f_send.at[0], f_recv.at[0], scen=scen_peer(k)).start()
        return carry

    lax.fori_loop(1, N_SCEN, send_q, 0)
    drain(QR.at[pl.ds(0, N_SCEN - 1)], f_recv.at[0])

    def send_all_q(k, carry):
        remote(QR, QA.at[i], f_send.at[1], f_recv.at[1], inst=inst_peer(k)).start()
        return carry

    lax.fori_loop(1, N_INST, send_all_q, 0)
    QA[i] = QR[...]
    q_copy = pltpu.make_async_copy(QR, qout, in_sem.at[5])
    q_copy.start()
    for h in range(2):
        drain(PNL.at[pl.ds(0, N_INST - 1), h], g_recv.at[h])
    drain(QA.at[pl.ds(0, N_INST - 1)], f_recv.at[1])

    for t in range(N_INST):
        place = jnp.where(c == t % 2, BOOKS // 2, 0) + (t // 2) * SHARE
        q = QA[t, :, 0, :][:, 0:1]
        for h in range(2):
            w = sigmoid((q - PNL[t, h]) * 2.0).astype(BF16)
            W[pl.ds(pl.multiple_of(place, SHARE), SHARE), pl.ds(h * HALF, HALF)] = w

    own_mass = QA[s, :, 0, :][:, 64:65]

    def sib_copy(n):
        return remote(SIBS.at[n], SIBR.at[n], sib_send.at[n], sib_recv.at[n], scen=z * 2 + (1 - c))

    def contribute(n):
        for u in range(2):
            width = CHUNK // 2
            cols = pl.ds(n * CHUNK + u * width, width)
            both = jnp.dot(W[...], PR[:, cols], preferred_element_type=F32)
            SIBS[n, :, pl.ds(u * width, width)] = both[: BOOKS // 2].astype(BF16)
            OWNC[n, :, pl.ds(u * width, width)] = both[BOOKS // 2 :]
        sib_copy(n).start()

    def ring_copy(n, way, step):
        if step == 0:
            cols = pl.ds(way * (CHUNK // 2), CHUNK // 2)
        else:
            cols = pl.ds(0, CHUNK)
        slot = (n * 2 + way) * 4 + step
        return remote(
            RSND.at[slot, :, cols], RRCV.at[slot, :, cols], r_send.at[slot], r_recv.at[slot],
            scen=ring_pos(1 if way == 0 else -1) * 2 + c,
        )

    def held(n, dest, cols):
        rows = pl.ds(pl.multiple_of(dest * SHARE, SHARE), SHARE)
        return OWNC[n, rows, cols] + SIBR[n, rows, cols].astype(F32)

    def ring_step(n, step):
        halves = (pl.ds(0, CHUNK // 2), pl.ds(CHUNK // 2, CHUNK // 2))
        if step == 4:
            ring_copy(n, 0, 3).wait_recv()
            ring_copy(n, 1, 3).wait_recv()
            total = held(n, z, pl.ds(0, CHUNK))
            total = total + RRCV[(n * 2) * 4 + 3].astype(F32) + RRCV[(n * 2 + 1) * 4 + 3].astype(F32)
            OUT[:, pl.ds(n * CHUNK, CHUNK)] = total / own_mass
            out_copy(n).start()
            return
        for way in range(2):
            slot = (n * 2 + way) * 4 + step
            dest = ring_pos((4 - step) * (1 if way == 0 else -1))
            if step == 0:
                RSND[slot, :, halves[way]] = held(n, dest, halves[way]).astype(BF16)
            else:
                ring_copy(n, way, step - 1).wait_recv()
                for u in range(2):
                    v = held(n, dest, halves[u])
                    if step > 1 or u == way:
                        v = v + RRCV[slot - 1, :, halves[u]].astype(F32)
                    RSND[slot, :, halves[u]] = v.astype(BF16)
            ring_copy(n, way, step).start()

    def out_copy(n):
        cols = pl.ds(n * CHUNK, CHUNK)
        return pltpu.make_async_copy(OUT.at[:, cols], out.at[:, cols], o_sem.at[n])

    for t in range(CHUNKS + 5):
        if t < CHUNKS:
            contribute(t)
        for n in range(CHUNKS):
            step = t - n - 1
            if step == 0:
                sib_copy(n).wait_recv()
            if 0 <= step <= 4:
                ring_step(n, step)

    drain(LH.at[pl.ds(0, SCEN_DEV * 15 // 16), :], a_send)
    for h in range(2):
        drain(RS.at[h, pl.ds(0, N_INST - 1)], c_send.at[h])
        drain(DV.at[h, pl.ds(0, N_SCEN - 1)], d_send.at[h])
        drain(PNL.at[pl.ds(0, N_INST - 1), h], g_send.at[h])
    drain(QR.at[pl.ds(0, N_SCEN - 1)], f_send.at[0])
    drain(QA.at[pl.ds(0, N_INST - 1)], f_send.at[1])
    q_copy.wait()
    for n in range(CHUNKS):
        sib_copy(n).wait_send()
        for way in range(2):
            for step in range(4):
                ring_copy(n, way, step).wait_send()
        out_copy(n).wait()


def body(shocks, loadings, delta, gamma, kappa, book_of, bracket_low, bracket_high, rank):
    anywhere = pl.BlockSpec(memory_space=pl.ANY)
    scalars = pl.BlockSpec(memory_space=pltpu.SMEM)
    row = lambda v: v.reshape(1, INST_DEV)
    dma = pltpu.SemaphoreType.DMA
    out, q = pl.pallas_call(
        kernel,
        out_shape=(
            jax.ShapeDtypeStruct((SHARE, INST_DEV), F32),
            jax.ShapeDtypeStruct((SHARE, 1, 128), F32),
        ),
        in_specs=[anywhere] * 6 + [scalars] * 3,
        out_specs=(anywhere, anywhere),
        scratch_shapes=[
            pltpu.VMEM((SCEN_DEV, FACTORS), BF16),
            pltpu.VMEM((TILES, FACTORS, TILE), BF16),
            pltpu.VMEM((SCEN_DEV, INST_DEV), BF16),
            pltpu.VMEM((BOOKS, INST_DEV), BF16),
            pltpu.VMEM((3, 1, INST_DEV), F32),
            pltpu.VMEM((1, INST_DEV), jnp.int32),
            pltpu.VMEM((2, BOOKS, HALF), F32),
            pltpu.VMEM((2, N_INST, SHARE, HALF), F32),
            pltpu.VMEM((2, SHARE, 2, 128), F32),
            pltpu.VMEM((2, N_SCEN, 2, 128), F32),
            pltpu.VMEM((N_INST, 2, SHARE, HALF), F32),
            pltpu.VMEM((SHARE, 1, 128), F32),
            pltpu.VMEM((N_INST, SHARE, 1, 128), F32),
            pltpu.VMEM((BOOKS, SCEN_DEV), BF16),
            pltpu.VMEM((CHUNKS, BOOKS // 2, CHUNK), BF16),
            pltpu.VMEM((CHUNKS, BOOKS // 2, CHUNK), BF16),
            pltpu.VMEM((CHUNKS, BOOKS // 2, CHUNK), F32),
            pltpu.VMEM((CHUNKS * 8, SHARE, CHUNK), BF16),
            pltpu.VMEM((CHUNKS * 8, SHARE, CHUNK), BF16),
            pltpu.VMEM((SHARE, INST_DEV), F32),
            dma((TILES,)),
            dma((6,)),
            dma(()),
            dma((80,)),
            dma((2,)), dma((2,)),
            dma((2,)), dma((2,)),
            dma((2,)), dma((2,)),
            dma((2,)), dma((2,)),
            dma((CHUNKS,)), dma((CHUNKS,)),
            dma((CHUNKS * 8,)), dma((CHUNKS * 8,)),
            dma((CHUNKS,)),
        ],
        compiler_params=pltpu.CompilerParams(
            collective_id=0, has_side_effects=True, vmem_limit_bytes=60 * 1024 * 1024
        ),
        name="revalue",
    )(
        shocks, loadings, row(delta), row(gamma), row(kappa), row(book_of),
        bracket_low, bracket_high, rank,
    )
    return out, q[:, 0, 0]


def solution(mesh):
    placed = (
        P("scen", "inst"),
        P(None, "inst"),
        P("inst"),
        P("inst"),
        P("inst"),
        P("inst"),
        P(),
        P(),
        P(),
    )
    return jax.shard_map(
        body, mesh=mesh, in_specs=placed, out_specs=(P("scen", "inst"), P("inst")), check_vma=False
    )
```

```python
import functools

import jax
import jax.numpy as jnp
from jax import lax
from jax.experimental import pallas as pl
from jax.experimental.pallas import tpu as pltpu
from jax.sharding import PartitionSpec as P

MESH = pl.DeviceIdType.MESH
F32 = jnp.float32
BF16 = jnp.bfloat16

PIVOTS = 64
ROUNDS = 3
BOOKS = 256
SIDE = 4
N_INST = 16
N_SCEN = 16
RING = 8
SHARE = 16
SCEN_DEV = 512
HALF = 256
FACT_DEV = 128
FACTORS = 2048
INST_DEV = 4096
TILE = 512
TILES = INST_DEV // TILE
CHUNKS = 4
CHUNK = INST_DEV // CHUNKS
PLACES = (
    (0, 0), (-1, 0), (1, 0), (0, -1), (0, 1),
    (-1, -1), (-1, 1), (1, -1), (1, 1), (2, 0), (0, 2),
    (2, -1), (2, 1), (-1, 2), (1, 2), (2, 2),
)
CUTS = (0, 4, 10, 16)
SCALE = (BOOKS / (INST_DEV * N_INST)) ** 0.5


def sigmoid(v):
    return 1.0 / (1.0 + jnp.exp(-v))


def kernel(
    shocks, loadings, delta, gamma, kappa, book_of, low, high, rank,
    out, qout,
    LH, LD, ACC, PR, OH, SENS, BK, PS, RS, ROWS, DV, PNL, QR, QA, W,
    SIBS, SIBR, OWNC, RSND, RRCV,
    ld_sem, in_sem, a_send, a_recv, c_send, c_recv, d_send, d_recv, g_send, g_recv,
    f_send, f_recv, sib_send, sib_recv, r_send, r_recv,
):
    s = lax.axis_index("scen")
    i = lax.axis_index("inst")
    x, y = lax.div(i, SIDE), lax.rem(i, SIDE)
    z, c = lax.div(s, 2), lax.rem(s, 2)

    def inst_at(dx, dy):
        return lax.rem(x + dx + SIDE, SIDE) * SIDE + lax.rem(y + dy + SIDE, SIDE)

    def inst_peer(k):
        return lax.rem(i + k, N_INST)

    def scen_peer(k):
        return lax.rem(s + k, N_SCEN)

    def ring_pos(d):
        return lax.rem(z + d + RING, RING)

    def remote(src, dst, ssem, rsem, **dev):
        return pltpu.make_async_remote_copy(
            src_ref=src, dst_ref=dst, send_sem=ssem, recv_sem=rsem,
            device_id=dev, device_id_type=MESH,
        )

    def drain(ref, sem):
        pltpu.make_async_copy(ref, ref, sem).wait()

    small = [
        pltpu.make_async_copy(shocks, LH.at[:, pl.ds(0, FACT_DEV)], in_sem.at[0]),
        pltpu.make_async_copy(delta, SENS.at[0], in_sem.at[1]),
        pltpu.make_async_copy(gamma, SENS.at[1], in_sem.at[2]),
        pltpu.make_async_copy(kappa, SENS.at[2], in_sem.at[3]),
        pltpu.make_async_copy(book_of, BK, in_sem.at[4]),
    ]
    for cp in small:
        cp.start()

    def load_block(p):
        source = inst_at(*PLACES[p])
        return pltpu.make_async_copy(
            loadings.at[pl.ds(pl.multiple_of(source * FACT_DEV, FACT_DEV), FACT_DEV), :],
            LD.at[pl.ds(p * FACT_DEV, FACT_DEV), :],
            ld_sem.at[p],
        )

    for p in range(N_INST):
        load_block(p).start()

    barrier = pltpu.get_barrier_semaphore()

    def greet(k, carry):
        pl.semaphore_signal(barrier, inc=1, device_id={"inst": inst_peer(k)}, device_id_type=MESH)
        pl.semaphore_signal(barrier, inc=1, device_id={"scen": scen_peer(k)}, device_id_type=MESH)
        return carry

    lax.fori_loop(1, 16, greet, 0)
    pl.semaphore_wait(barrier, 30)

    def along(colour, first, second):
        return inst_at(first, second) if colour == 0 else inst_at(second, first)

    def place_of(colour, a, b):
        fold = lambda v: (v + 1) % SIDE - 1
        return PLACES.index((fold(a), fold(b)) if colour == 0 else (fold(b), fold(a)))

    def rows_of(colour, part):
        start, size = colour * HALF, HALF
        if part:
            size //= 2
            start += size * (part - 1)
        return pl.ds(start, size)

    def piece(colour, a, b, part):
        return LH.at[rows_of(colour, part), pl.ds(place_of(colour, a, b) * FACT_DEV, FACT_DEV)]

    def a_pass(colour, a, b, part, first, second, pid):
        if (a, b) == (0, 0):
            src = shocks.at[rows_of(colour, part), :]
        else:
            src = piece(colour, a, b, part)
        remote(
            src, piece(colour, a - first, b - second, part), a_send, a_recv.at[colour * 20 + pid],
            inst=along(colour, first, second),
        ).start()

    def a_wait(colour, a, b, part, pid):
        drain(piece(colour, a, b, part), a_recv.at[colour * 20 + pid])

    lanes = (0, -1, 1, 2)

    def a_second(colour, q):
        a_pass(colour, lanes[q], 0, 0, 0, 1, 4 + 4 * q)
        a_pass(colour, lanes[q], 0, 0, 0, -1, 5 + 4 * q)

    def a_hand_on(colour, q):
        a_wait(colour, lanes[q], -1, 0, 4 + 4 * q)
        a_pass(colour, lanes[q], -1, 1, 0, 1, 6 + 4 * q)
        a_wait(colour, lanes[q], 1, 0, 5 + 4 * q)
        a_pass(colour, lanes[q], 1, 2, 0, -1, 7 + 4 * q)

    def a_last(colour, q):
        a_wait(colour, lanes[q], 2, 1, 6 + 4 * q)
        a_wait(colour, lanes[q], 2, 2, 7 + 4 * q)

    def a_step(step):
        for colour in range(2):
            if step == 0:
                a_pass(colour, 0, 0, 0, 1, 0, 0)
                a_pass(colour, 0, 0, 0, -1, 0, 1)
                a_second(colour, 0)
            elif step == 1:
                a_wait(colour, -1, 0, 0, 0)
                a_pass(colour, -1, 0, 1, 1, 0, 2)
                a_second(colour, 1)
                a_wait(colour, 1, 0, 0, 1)
                a_pass(colour, 1, 0, 2, -1, 0, 3)
                a_second(colour, 2)
            elif step == 2:
                a_hand_on(colour, 0)
            elif step == 3:
                a_wait(colour, 2, 0, 1, 2)
                a_wait(colour, 2, 0, 2, 3)
                a_second(colour, 3)
            elif step == 4:
                a_hand_on(colour, 1)
                a_hand_on(colour, 2)
                a_last(colour, 0)
            elif step == 5:
                a_hand_on(colour, 3)
            else:
                for q in range(1, 4):
                    a_last(colour, q)

    a_step(0)
    small[4].wait()
    book_ids = lax.broadcasted_iota(jnp.int32, (BOOKS, TILE), 0)

    def one_hot(n, carry):
        cols = pl.ds(pl.multiple_of(n * TILE, TILE), TILE)
        OH[:, cols] = jnp.where(BK[:, cols] == book_ids, 1.0, 0.0).astype(BF16)
        return carry

    lax.fori_loop(0, TILES, one_hot, 0)
    PS[...] = jnp.zeros_like(PS)
    a_step(1)
    a_step(2)
    for cp in small[:4]:
        cp.wait()

    def share_rows(k):
        return pl.ds(pl.multiple_of(k * SHARE, SHARE), SHARE)

    def send_sums(h):
        def one(k, carry):
            p = inst_peer(k)
            remote(PS.at[h, share_rows(p), :], RS.at[h, i], c_send.at[h], c_recv.at[h], inst=p).start()
            return carry

        lax.fori_loop(1, N_INST, one, 0)
        RS[h, i] = PS[h, share_rows(i), :]

    def take_sums(h):
        drain(RS.at[h, pl.ds(0, N_INST - 1)], c_recv.at[h])
        total = RS[h, 0]
        for k in range(1, N_INST):
            total = total + RS[h, k]
        total = total * SCALE
        PNL[i, h] = total
        for r in range(2):
            ROWS[h, :, r, :] = total[:, r * 128 : (r + 1) * 128]

        def one(k, carry):
            p = scen_peer(k)
            remote(ROWS.at[h, p], DV.at[h, s], d_send.at[h], d_recv.at[h], scen=p).start()
            return carry

        lax.fori_loop(1, N_SCEN, one, 0)

        def other(k, carry):
            p = inst_peer(k)
            remote(PNL.at[i, h], PNL.at[i, h], g_send.at[h], g_recv.at[h], inst=p).start()
            return carry

        lax.fori_loop(1, N_INST, other, 0)
        DV[h, s] = ROWS[h, s]

    def factors(group):
        return pl.ds(CUTS[group] * FACT_DEV, (CUTS[group + 1] - CUTS[group]) * FACT_DEV)

    def wait_blocks(group):
        for p in range(CUTS[group], CUTS[group + 1]):
            load_block(p).wait()

    def tile_cols(n):
        return pl.ds(pl.multiple_of(n * TILE, TILE), TILE)

    def first_group(n, carry):
        cols = tile_cols(n)
        ACC[:, cols] = jnp.dot(LH[:, factors(0)], LD[factors(0), cols], preferred_element_type=F32)
        return carry

    def second_group(n, carry):
        cols = tile_cols(n)
        ACC[:, cols] += jnp.dot(LH[:, factors(1)], LD[factors(1), cols], preferred_element_type=F32)

        @pl.when(n == 4)
        def _():
            a_step(5)

        return carry

    def last_group(h, n):
        cols = tile_cols(n)
        rows = pl.ds(h * HALF, HALF)
        moves = ACC[rows, cols] + jnp.dot(LH[rows, factors(2)], LD[factors(2), cols], preferred_element_type=F32)
        d, g, k = SENS[0, :, cols], SENS[1, :, cols], SENS[2, :, cols]
        profit = (moves * (d + moves * (g + moves * k))).astype(BF16)
        PR[rows, cols] = profit
        part = lax.dot_general(OH[:, cols], profit, (((1,), (1,)), ((), ())), preferred_element_type=F32)
        PS[h] += part

    def last_first(n, carry):
        last_group(0, n)
        return carry

    def last_second(n, carry):
        last_group(1, n)
        return carry

    wait_blocks(0)
    lax.fori_loop(0, TILES, first_group, 0)
    a_step(3)
    a_step(4)
    wait_blocks(1)
    lax.fori_loop(0, TILES, second_group, 0)
    a_step(6)
    wait_blocks(2)
    lax.fori_loop(0, TILES, last_first, 0)
    send_sums(0)
    lax.fori_loop(0, TILES, last_second, 0)
    send_sums(1)
    take_sums(0)
    take_sums(1)

    book = i * SHARE + s
    lower = jnp.full((PIVOTS, 128), low[book], jnp.int32).astype(F32) * 0.125
    upper = jnp.full((PIVOTS, 128), high[book], jnp.int32).astype(F32) * 0.125
    wanted = jnp.full((PIVOTS, 128), rank[book], jnp.int32).astype(F32)
    levels = lax.broadcasted_iota(jnp.int32, (PIVOTS, 128), 0).astype(F32)
    for h in range(2):
        drain(DV.at[h, pl.ds(0, N_SCEN - 1)], d_recv.at[h])
    for _ in range(ROUNDS):
        spacing = (upper - lower) / (PIVOTS - 1)
        marks = lower + levels * spacing
        count = jnp.zeros((PIVOTS, 128), F32)
        for h in range(2):
            for p in range(N_SCEN):
                for r in range(2):
                    row = DV[h, p, pl.ds(r, 1), :]
                    count = count + jnp.where(row <= marks, 1.0, 0.0)
        count = jnp.sum(count, axis=1, keepdims=True)
        below = jnp.sum(jnp.where(count < wanted, 1.0, 0.0), axis=0, keepdims=True)
        chosen = jnp.clip(below, 1.0, PIVOTS - 1.0)
        upper = lower + chosen * spacing
        lower = lower + (chosen - 1.0) * spacing
    quantile = (lower + upper) * 0.5
    pair_q = quantile[0:2, :]
    mass = jnp.zeros((2, 128), F32)
    for h in range(2):
        for p in range(N_SCEN):
            mass = mass + sigmoid((pair_q - DV[h, p]) * 2.0).astype(BF16).astype(F32)
    mass = jnp.sum(jnp.sum(mass, axis=1, keepdims=True), axis=0, keepdims=True)
    lane = lax.broadcasted_iota(jnp.int32, (1, 128), 1)
    QR[s] = jnp.where(lane < 64, quantile[0:1, :], jnp.broadcast_to(mass, (1, 128)))

    def send_q(k, carry):
        remote(QR.at[s], QR.at[s], f_send.at[0], f_recv.at[0], scen=scen_peer(k)).start()
        return carry

    lax.fori_loop(1, N_SCEN, send_q, 0)
    drain(QR.at[pl.ds(0, N_SCEN - 1)], f_recv.at[0])

    def send_all_q(k, carry):
        remote(QR, QA.at[i], f_send.at[1], f_recv.at[1], inst=inst_peer(k)).start()
        return carry

    lax.fori_loop(1, N_INST, send_all_q, 0)
    QA[i] = QR[...]
    qout[...] = QR[...]
    for h in range(2):
        drain(PNL.at[pl.ds(0, N_INST - 1), h], g_recv.at[h])
    drain(QA.at[pl.ds(0, N_INST - 1)], f_recv.at[1])

    for t in range(N_INST):
        place = jnp.where(c == t % 2, BOOKS // 2, 0) + (t // 2) * SHARE
        q = QA[t, :, 0, :][:, 0:1]
        for h in range(2):
            w = sigmoid((q - PNL[t, h]) * 2.0).astype(BF16)
            W[pl.ds(pl.multiple_of(place, SHARE), SHARE), pl.ds(h * HALF, HALF)] = w

    own_mass = QA[s, :, 0, :][:, 64:65]

    def sib_copy(n):
        return remote(SIBS.at[n], SIBR.at[n], sib_send.at[n], sib_recv.at[n], scen=z * 2 + (1 - c))

    def contribute(n):
        for u in range(2):
            width = CHUNK // 2
            cols = pl.ds(n * CHUNK + u * width, width)
            both = jnp.dot(W[...], PR[:, cols], preferred_element_type=F32)
            SIBS[n, :, pl.ds(u * width, width)] = both[: BOOKS // 2].astype(BF16)
            OWNC[n, :, pl.ds(u * width, width)] = both[BOOKS // 2 :]
        sib_copy(n).start()

    def ring_copy(n, way, step):
        if step == 0:
            cols = pl.ds(way * (CHUNK // 2), CHUNK // 2)
        else:
            cols = pl.ds(0, CHUNK)
        slot = (n * 2 + way) * 4 + step
        return remote(
            RSND.at[slot, :, cols], RRCV.at[slot, :, cols], r_send.at[slot], r_recv.at[slot],
            scen=ring_pos(1 if way == 0 else -1) * 2 + c,
        )

    def held(n, dest, cols):
        rows = pl.ds(pl.multiple_of(dest * SHARE, SHARE), SHARE)
        return OWNC[n, rows, cols] + SIBR[n, rows, cols].astype(F32)

    def ring_step(n, step):
        halves = (pl.ds(0, CHUNK // 2), pl.ds(CHUNK // 2, CHUNK // 2))
        if step == 4:
            ring_copy(n, 0, 3).wait_recv()
            ring_copy(n, 1, 3).wait_recv()
            total = held(n, z, pl.ds(0, CHUNK))
            total = total + RRCV[(n * 2) * 4 + 3].astype(F32) + RRCV[(n * 2 + 1) * 4 + 3].astype(F32)
            out[:, pl.ds(n * CHUNK, CHUNK)] = total / own_mass
            return
        for way in range(2):
            slot = (n * 2 + way) * 4 + step
            dest = ring_pos((4 - step) * (1 if way == 0 else -1))
            if step == 0:
                RSND[slot, :, halves[way]] = held(n, dest, halves[way]).astype(BF16)
            else:
                ring_copy(n, way, step - 1).wait_recv()
                for u in range(2):
                    v = held(n, dest, halves[u])
                    if step > 1 or u == way:
                        v = v + RRCV[slot - 1, :, halves[u]].astype(F32)
                    RSND[slot, :, halves[u]] = v.astype(BF16)
            ring_copy(n, way, step).start()

    for n in range(CHUNKS):
        contribute(n)
    for n in range(CHUNKS):
        sib_copy(n).wait_recv()
        ring_step(n, 0)
    for n in range(CHUNKS):
        ring_step(n, 1)
    for n in range(CHUNKS):
        ring_step(n, 2)
    for n in range(CHUNKS):
        ring_step(n, 3)
    for n in range(CHUNKS):
        ring_step(n, 4)

    drain(LH.at[pl.ds(0, SCEN_DEV * 15 // 16), :], a_send)
    for h in range(2):
        drain(RS.at[h, pl.ds(0, N_INST - 1)], c_send.at[h])
        drain(DV.at[h, pl.ds(0, N_SCEN - 1)], d_send.at[h])
        drain(PNL.at[pl.ds(0, N_INST - 1), h], g_send.at[h])
    drain(QR.at[pl.ds(0, N_SCEN - 1)], f_send.at[0])
    drain(QA.at[pl.ds(0, N_INST - 1)], f_send.at[1])
    for n in range(CHUNKS):
        sib_copy(n).wait_send()
        for way in range(2):
            for step in range(4):
                ring_copy(n, way, step).wait_send()


def body(shocks, loadings, delta, gamma, kappa, book_of, bracket_low, bracket_high, rank):
    anywhere = pl.BlockSpec(memory_space=pl.ANY)
    scalars = pl.BlockSpec(memory_space=pltpu.SMEM)
    row = lambda v: v.reshape(1, INST_DEV)
    dma = pltpu.SemaphoreType.DMA
    out, q = pl.pallas_call(
        kernel,
        out_shape=(
            jax.ShapeDtypeStruct((SHARE, INST_DEV), F32),
            jax.ShapeDtypeStruct((SHARE, 1, 128), F32),
        ),
        in_specs=[anywhere] * 6 + [scalars] * 3,
        out_specs=(pl.BlockSpec(memory_space=pltpu.VMEM),) * 2,
        scratch_shapes=[
            pltpu.VMEM((SCEN_DEV, FACTORS), BF16),
            pltpu.VMEM((FACTORS, INST_DEV), BF16),
            pltpu.VMEM((SCEN_DEV, INST_DEV), F32),
            pltpu.VMEM((SCEN_DEV, INST_DEV), BF16),
            pltpu.VMEM((BOOKS, INST_DEV), BF16),
            pltpu.VMEM((3, 1, INST_DEV), F32),
            pltpu.VMEM((1, INST_DEV), jnp.int32),
            pltpu.VMEM((2, BOOKS, HALF), F32),
            pltpu.VMEM((2, N_INST, SHARE, HALF), F32),
            pltpu.VMEM((2, SHARE, 2, 128), F32),
            pltpu.VMEM((2, N_SCEN, 2, 128), F32),
            pltpu.VMEM((N_INST, 2, SHARE, HALF), F32),
            pltpu.VMEM((SHARE, 1, 128), F32),
            pltpu.VMEM((N_INST, SHARE, 1, 128), F32),
            pltpu.VMEM((BOOKS, SCEN_DEV), BF16),
            pltpu.VMEM((CHUNKS, BOOKS // 2, CHUNK), BF16),
            pltpu.VMEM((CHUNKS, BOOKS // 2, CHUNK), BF16),
            pltpu.VMEM((CHUNKS, BOOKS // 2, CHUNK), F32),
            pltpu.VMEM((CHUNKS * 8, SHARE, CHUNK), BF16),
            pltpu.VMEM((CHUNKS * 8, SHARE, CHUNK), BF16),
            dma((N_INST,)),
            dma((5,)),
            dma(()),
            dma((40,)),
            dma((2,)), dma((2,)),
            dma((2,)), dma((2,)),
            dma((2,)), dma((2,)),
            dma((2,)), dma((2,)),
            dma((CHUNKS,)), dma((CHUNKS,)),
            dma((CHUNKS * 8,)), dma((CHUNKS * 8,)),
        ],
        compiler_params=pltpu.CompilerParams(
            collective_id=0, has_side_effects=True, vmem_limit_bytes=60 * 1024 * 1024
        ),
        name="revalue",
    )(
        shocks, loadings, row(delta), row(gamma), row(kappa), row(book_of),
        bracket_low, bracket_high, rank,
    )
    return out, q[:, 0, 0]


def solution(mesh):
    placed = (
        P("scen", "inst"),
        P(None, "inst"),
        P("inst"),
        P("inst"),
        P("inst"),
        P("inst"),
        P(),
        P(),
        P(),
    )
    return jax.shard_map(
        body, mesh=mesh, in_specs=placed, out_specs=(P("scen", "inst"), P("inst")), check_vma=False
    )
```

```python
import functools

import jax
import jax.numpy as jnp
from jax import lax
from jax.experimental import pallas as pl
from jax.experimental.pallas import tpu as pltpu
from jax.sharding import PartitionSpec as P

MESH = pl.DeviceIdType.MESH
F32 = jnp.float32
BF16 = jnp.bfloat16

PIVOTS = 64
ROUNDS = 3
BOOKS = 256
SIDE = 4
N_INST = 16
N_SCEN = 16
RING = 8
SHARE = 16
SCEN_DEV = 512
HALF = 256
FACT_DEV = 128
FACTORS = 2048
INST_DEV = 4096
TILE = 1024
TILES = INST_DEV // TILE
CHUNKS = 4
CHUNK = INST_DEV // CHUNKS
PLACES = (
    (0, 0), (-1, 0), (1, 0), (0, -1), (0, 1),
    (-1, -1), (-1, 1), (1, -1), (1, 1), (2, 0), (0, 2),
    (2, -1), (2, 1), (-1, 2), (1, 2), (2, 2),
)
CUTS = (0, 4, 10, 16)
SCALE = (BOOKS / (INST_DEV * N_INST)) ** 0.5


def sigmoid(v):
    return 1.0 / (1.0 + jnp.exp(-v))


def kernel(
    shocks, loadings, delta, gamma, kappa, book_of, low, high, rank,
    out, qout,
    LH, LD, ACC, PR, OH, SENS, BK, ST, PS, RS, ROWS, DV, PNL, QR, QA, W,
    SIBS, SIBR, OWNC, RSND, RRCV,
    ld_sem, in_sem, a_send, a_recv, c_send, c_recv, d_send, d_recv, g_send, g_recv,
    f_send, f_recv, sib_send, sib_recv, r_send, r_recv,
):
    s = lax.axis_index("scen")
    i = lax.axis_index("inst")
    x, y = lax.div(i, SIDE), lax.rem(i, SIDE)
    z, c = lax.div(s, 2), lax.rem(s, 2)

    def inst_at(dx, dy):
        return lax.rem(x + dx + SIDE, SIDE) * SIDE + lax.rem(y + dy + SIDE, SIDE)

    def inst_peer(k):
        return lax.rem(i + k, N_INST)

    def scen_peer(k):
        return lax.rem(s + k, N_SCEN)

    def ring_pos(d):
        return lax.rem(z + d + RING, RING)

    def remote(src, dst, ssem, rsem, **dev):
        return pltpu.make_async_remote_copy(
            src_ref=src, dst_ref=dst, send_sem=ssem, recv_sem=rsem,
            device_id=dev, device_id_type=MESH,
        )

    def drain(ref, sem):
        pltpu.make_async_copy(ref, ref, sem).wait()

    small = [
        pltpu.make_async_copy(shocks, LH.at[:, pl.ds(0, FACT_DEV)], in_sem.at[0]),
        pltpu.make_async_copy(delta, SENS.at[0], in_sem.at[1]),
        pltpu.make_async_copy(gamma, SENS.at[1], in_sem.at[2]),
        pltpu.make_async_copy(kappa, SENS.at[2], in_sem.at[3]),
        pltpu.make_async_copy(book_of, BK, in_sem.at[4]),
    ]
    for cp in small:
        cp.start()

    def load_block(p):
        source = inst_at(*PLACES[p])
        return pltpu.make_async_copy(
            loadings.at[pl.ds(pl.multiple_of(source * FACT_DEV, FACT_DEV), FACT_DEV), :],
            LD.at[pl.ds(p * FACT_DEV, FACT_DEV), :],
            ld_sem.at[p],
        )

    for p in range(N_INST):
        load_block(p).start()

    barrier = pltpu.get_barrier_semaphore()

    def greet(k, carry):
        pl.semaphore_signal(barrier, inc=1, device_id={"inst": inst_peer(k)}, device_id_type=MESH)
        pl.semaphore_signal(barrier, inc=1, device_id={"scen": scen_peer(k)}, device_id_type=MESH)
        return carry

    lax.fori_loop(1, 16, greet, 0)
    pl.semaphore_wait(barrier, 30)

    def along(colour, first, second):
        return inst_at(first, second) if colour == 0 else inst_at(second, first)

    def place_of(colour, a, b):
        fold = lambda v: (v + 1) % SIDE - 1
        return PLACES.index((fold(a), fold(b)) if colour == 0 else (fold(b), fold(a)))

    def rows_of(colour, part):
        start, size = colour * HALF, HALF
        if part:
            size //= 2
            start += size * (part - 1)
        return pl.ds(start, size)

    def piece(colour, a, b, part):
        return LH.at[rows_of(colour, part), pl.ds(place_of(colour, a, b) * FACT_DEV, FACT_DEV)]

    def a_pass(colour, a, b, part, first, second, pid):
        if (a, b) == (0, 0):
            src = shocks.at[rows_of(colour, part), :]
        else:
            src = piece(colour, a, b, part)
        remote(
            src, piece(colour, a - first, b - second, part), a_send, a_recv.at[colour * 20 + pid],
            inst=along(colour, first, second),
        ).start()

    def a_wait(colour, a, b, part, pid):
        drain(piece(colour, a, b, part), a_recv.at[colour * 20 + pid])

    lanes = (0, -1, 1, 2)

    def a_second(colour, q):
        a_pass(colour, lanes[q], 0, 0, 0, 1, 4 + 4 * q)
        a_pass(colour, lanes[q], 0, 0, 0, -1, 5 + 4 * q)

    def a_hand_on(colour, q):
        a_wait(colour, lanes[q], -1, 0, 4 + 4 * q)
        a_pass(colour, lanes[q], -1, 1, 0, 1, 6 + 4 * q)
        a_wait(colour, lanes[q], 1, 0, 5 + 4 * q)
        a_pass(colour, lanes[q], 1, 2, 0, -1, 7 + 4 * q)

    def a_last(colour, q):
        a_wait(colour, lanes[q], 2, 1, 6 + 4 * q)
        a_wait(colour, lanes[q], 2, 2, 7 + 4 * q)

    def a_step(step):
        for colour in range(2):
            if step == 0:
                a_pass(colour, 0, 0, 0, 1, 0, 0)
                a_pass(colour, 0, 0, 0, -1, 0, 1)
                a_second(colour, 0)
            elif step == 1:
                a_wait(colour, -1, 0, 0, 0)
                a_pass(colour, -1, 0, 1, 1, 0, 2)
                a_second(colour, 1)
                a_wait(colour, 1, 0, 0, 1)
                a_pass(colour, 1, 0, 2, -1, 0, 3)
                a_second(colour, 2)
            elif step == 2:
                a_hand_on(colour, 0)
            elif step == 3:
                a_wait(colour, 2, 0, 1, 2)
                a_wait(colour, 2, 0, 2, 3)
                a_second(colour, 3)
            elif step == 4:
                a_hand_on(colour, 1)
                a_hand_on(colour, 2)
                a_last(colour, 0)
            elif step == 5:
                a_hand_on(colour, 3)
            else:
                for q in range(1, 4):
                    a_last(colour, q)

    a_step(0)
    small[4].wait()
    book_ids = lax.broadcasted_iota(jnp.int32, (BOOKS, TILE), 0)

    def one_hot(n, carry):
        cols = pl.ds(pl.multiple_of(n * TILE, TILE), TILE)
        OH[cols, :] = jnp.transpose(jnp.where(BK[:, cols] == book_ids, 1.0, 0.0).astype(BF16))
        return carry

    lax.fori_loop(0, TILES, one_hot, 0)
    ST[...] = jnp.zeros_like(ST)
    a_step(1)
    a_step(2)
    for cp in small[:4]:
        cp.wait()

    def share_rows(k):
        return pl.ds(pl.multiple_of(k * SHARE, SHARE), SHARE)

    def send_sums(h):
        PS[h] = jnp.transpose(ST[h])

        def one(k, carry):
            p = inst_peer(k)
            remote(PS.at[h, share_rows(p), :], RS.at[h, i], c_send.at[h], c_recv.at[h], inst=p).start()
            return carry

        lax.fori_loop(1, N_INST, one, 0)
        RS[h, i] = PS[h, share_rows(i), :]

    def take_sums(h):
        drain(RS.at[h, pl.ds(0, N_INST - 1)], c_recv.at[h])
        total = RS[h, 0]
        for k in range(1, N_INST):
            total = total + RS[h, k]
        total = total * SCALE
        PNL[i, h] = total
        for r in range(2):
            ROWS[h, :, r, :] = total[:, r * 128 : (r + 1) * 128]

        def one(k, carry):
            p = scen_peer(k)
            remote(ROWS.at[h, p], DV.at[h, s], d_send.at[h], d_recv.at[h], scen=p).start()
            return carry

        lax.fori_loop(1, N_SCEN, one, 0)

        def other(k, carry):
            p = inst_peer(k)
            remote(PNL.at[i, h], PNL.at[i, h], g_send.at[h], g_recv.at[h], inst=p).start()
            return carry

        lax.fori_loop(1, N_INST, other, 0)
        DV[h, s] = ROWS[h, s]

    def factors(group):
        return pl.ds(CUTS[group] * FACT_DEV, (CUTS[group + 1] - CUTS[group]) * FACT_DEV)

    def wait_blocks(group):
        for p in range(CUTS[group], CUTS[group + 1]):
            load_block(p).wait()

    def tile_cols(n):
        return pl.ds(pl.multiple_of(n * TILE, TILE), TILE)

    def first_group(n, carry):
        cols = tile_cols(n)
        ACC[:, cols] = jnp.dot(LH[:, factors(0)], LD[factors(0), cols], preferred_element_type=F32)
        return carry

    def second_group(n, carry):
        cols = tile_cols(n)
        ACC[:, cols] += jnp.dot(LH[:, factors(1)], LD[factors(1), cols], preferred_element_type=F32)

        @pl.when(n == TILES // 2)
        def _():
            a_step(5)

        return carry

    def last_group(h, n):
        cols = tile_cols(n)
        rows = pl.ds(h * HALF, HALF)
        moves = ACC[rows, cols] + jnp.dot(LH[rows, factors(2)], LD[factors(2), cols], preferred_element_type=F32)
        d, g, k = SENS[0, :, cols], SENS[1, :, cols], SENS[2, :, cols]
        profit = (moves * (d + moves * (g + moves * k))).astype(BF16)
        PR[rows, cols] = profit
        ST[h] += jnp.dot(profit, OH[cols, :], preferred_element_type=F32)

    def last_first(n, carry):
        last_group(0, n)
        return carry

    def last_second(n, carry):
        last_group(1, n)
        return carry

    wait_blocks(0)
    lax.fori_loop(0, TILES, first_group, 0)
    a_step(3)
    a_step(4)
    wait_blocks(1)
    lax.fori_loop(0, TILES, second_group, 0)
    a_step(6)
    wait_blocks(2)
    lax.fori_loop(0, TILES, last_first, 0)
    send_sums(0)
    lax.fori_loop(0, TILES, last_second, 0)
    send_sums(1)
    take_sums(0)
    take_sums(1)

    book = i * SHARE + s
    lower = jnp.full((PIVOTS, 128), low[book], jnp.int32).astype(F32) * 0.125
    upper = jnp.full((PIVOTS, 128), high[book], jnp.int32).astype(F32) * 0.125
    wanted = jnp.full((PIVOTS, 128), rank[book], jnp.int32).astype(F32)
    levels = lax.broadcasted_iota(jnp.int32, (PIVOTS, 128), 0).astype(F32)
    for h in range(2):
        drain(DV.at[h, pl.ds(0, N_SCEN - 1)], d_recv.at[h])
    for _ in range(ROUNDS):
        spacing = (upper - lower) / (PIVOTS - 1)
        marks = lower + levels * spacing
        count = jnp.zeros((PIVOTS, 128), F32)
        for h in range(2):
            for p in range(N_SCEN):
                for r in range(2):
                    row = DV[h, p, pl.ds(r, 1), :]
                    count = count + jnp.where(row <= marks, 1.0, 0.0)
        count = jnp.sum(count, axis=1, keepdims=True)
        below = jnp.sum(jnp.where(count < wanted, 1.0, 0.0), axis=0, keepdims=True)
        chosen = jnp.clip(below, 1.0, PIVOTS - 1.0)
        upper = lower + chosen * spacing
        lower = lower + (chosen - 1.0) * spacing
    quantile = (lower + upper) * 0.5
    pair_q = quantile[0:2, :]
    mass = jnp.zeros((2, 128), F32)
    for h in range(2):
        for p in range(N_SCEN):
            mass = mass + sigmoid((pair_q - DV[h, p]) * 2.0).astype(BF16).astype(F32)
    mass = jnp.sum(jnp.sum(mass, axis=1, keepdims=True), axis=0, keepdims=True)
    lane = lax.broadcasted_iota(jnp.int32, (1, 128), 1)
    QR[s] = jnp.where(lane < 64, quantile[0:1, :], jnp.broadcast_to(mass, (1, 128)))

    def send_q(k, carry):
        remote(QR.at[s], QR.at[s], f_send.at[0], f_recv.at[0], scen=scen_peer(k)).start()
        return carry

    lax.fori_loop(1, N_SCEN, send_q, 0)
    drain(QR.at[pl.ds(0, N_SCEN - 1)], f_recv.at[0])

    def send_all_q(k, carry):
        remote(QR, QA.at[i], f_send.at[1], f_recv.at[1], inst=inst_peer(k)).start()
        return carry

    lax.fori_loop(1, N_INST, send_all_q, 0)
    QA[i] = QR[...]
    books = lax.broadcasted_iota(jnp.int32, (SHARE, 128), 0)
    lanes_q = lax.broadcasted_iota(jnp.int32, (SHARE, 128), 1)
    qout[...] = jnp.sum(jnp.where(books == lanes_q, QR[:, 0, :], 0.0), axis=0)[:SHARE]
    for h in range(2):
        drain(PNL.at[pl.ds(0, N_INST - 1), h], g_recv.at[h])
    drain(QA.at[pl.ds(0, N_INST - 1)], f_recv.at[1])

    for t in range(N_INST):
        place = jnp.where(c == t % 2, BOOKS // 2, 0) + (t // 2) * SHARE
        q = QA[t, :, 0, :][:, 0:1]
        for h in range(2):
            w = sigmoid((q - PNL[t, h]) * 2.0).astype(BF16)
            W[pl.ds(pl.multiple_of(place, SHARE), SHARE), pl.ds(h * HALF, HALF)] = w

    own_mass = QA[s, :, 0, :][:, 64:65]

    def sib_copy(n):
        return remote(SIBS.at[n], SIBR.at[n], sib_send.at[n], sib_recv.at[n], scen=z * 2 + (1 - c))

    def contribute(n):
        for u in range(2):
            width = CHUNK // 2
            cols = pl.ds(n * CHUNK + u * width, width)
            both = jnp.dot(W[...], PR[:, cols], preferred_element_type=F32)
            SIBS[n, :, pl.ds(u * width, width)] = both[: BOOKS // 2].astype(BF16)
            OWNC[n, :, pl.ds(u * width, width)] = both[BOOKS // 2 :]
        sib_copy(n).start()

    def ring_copy(n, way, step):
        if step == 0:
            cols = pl.ds(way * (CHUNK // 2), CHUNK // 2)
        else:
            cols = pl.ds(0, CHUNK)
        slot = (n * 2 + way) * 4 + step
        return remote(
            RSND.at[slot, :, cols], RRCV.at[slot, :, cols], r_send.at[slot], r_recv.at[slot],
            scen=ring_pos(1 if way == 0 else -1) * 2 + c,
        )

    def held(n, dest, cols):
        rows = pl.ds(pl.multiple_of(dest * SHARE, SHARE), SHARE)
        return OWNC[n, rows, cols] + SIBR[n, rows, cols].astype(F32)

    def ring_step(n, step):
        halves = (pl.ds(0, CHUNK // 2), pl.ds(CHUNK // 2, CHUNK // 2))
        if step == 4:
            ring_copy(n, 0, 3).wait_recv()
            ring_copy(n, 1, 3).wait_recv()
            total = held(n, z, pl.ds(0, CHUNK))
            total = total + RRCV[(n * 2) * 4 + 3].astype(F32) + RRCV[(n * 2 + 1) * 4 + 3].astype(F32)
            out[:, pl.ds(n * CHUNK, CHUNK)] = total / own_mass
            return
        for way in range(2):
            slot = (n * 2 + way) * 4 + step
            dest = ring_pos((4 - step) * (1 if way == 0 else -1))
            if step == 0:
                RSND[slot, :, halves[way]] = held(n, dest, halves[way]).astype(BF16)
            else:
                ring_copy(n, way, step - 1).wait_recv()
                for u in range(2):
                    v = held(n, dest, halves[u])
                    if step > 1 or u == way:
                        v = v + RRCV[slot - 1, :, halves[u]].astype(F32)
                    RSND[slot, :, halves[u]] = v.astype(BF16)
            ring_copy(n, way, step).start()

    def first_step(n):
        sib_copy(n).wait_recv()
        ring_step(n, 0)

    for n in range(CHUNKS):
        contribute(n)
        if n > 1:
            first_step(n - 2)
    first_step(CHUNKS - 2)
    first_step(CHUNKS - 1)
    for n in range(CHUNKS):
        ring_step(n, 1)
    for n in range(CHUNKS):
        ring_step(n, 2)
    for n in range(CHUNKS):
        ring_step(n, 3)
    for n in range(CHUNKS):
        ring_step(n, 4)

    drain(LH.at[pl.ds(0, SCEN_DEV * 15 // 16), :], a_send)
    for h in range(2):
        drain(RS.at[h, pl.ds(0, N_INST - 1)], c_send.at[h])
        drain(DV.at[h, pl.ds(0, N_SCEN - 1)], d_send.at[h])
        drain(PNL.at[pl.ds(0, N_INST - 1), h], g_send.at[h])
    drain(QR.at[pl.ds(0, N_SCEN - 1)], f_send.at[0])
    drain(QA.at[pl.ds(0, N_INST - 1)], f_send.at[1])
    for n in range(CHUNKS):
        sib_copy(n).wait_send()
        for way in range(2):
            for step in range(4):
                ring_copy(n, way, step).wait_send()


def body(shocks, loadings, delta, gamma, kappa, book_of, bracket_low, bracket_high, rank):
    anywhere = pl.BlockSpec(memory_space=pl.ANY)
    scalars = pl.BlockSpec(memory_space=pltpu.SMEM)
    row = lambda v: v.reshape(1, INST_DEV)
    dma = pltpu.SemaphoreType.DMA
    out, q = pl.pallas_call(
        kernel,
        out_shape=(
            pltpu.VMEM((SHARE, INST_DEV), F32),
            pltpu.VMEM((SHARE,), F32),
        ),
        in_specs=[anywhere] * 6 + [scalars] * 3,
        out_specs=(pl.BlockSpec(memory_space=pltpu.VMEM),) * 2,
        scratch_shapes=[
            pltpu.VMEM((SCEN_DEV, FACTORS), BF16),
            pltpu.VMEM((FACTORS, INST_DEV), BF16),
            pltpu.VMEM((SCEN_DEV, INST_DEV), F32),
            pltpu.VMEM((SCEN_DEV, INST_DEV), BF16),
            pltpu.VMEM((INST_DEV, BOOKS), BF16),
            pltpu.VMEM((3, 1, INST_DEV), F32),
            pltpu.VMEM((1, INST_DEV), jnp.int32),
            pltpu.VMEM((2, HALF, BOOKS), F32),
            pltpu.VMEM((2, BOOKS, HALF), F32),
            pltpu.VMEM((2, N_INST, SHARE, HALF), F32),
            pltpu.VMEM((2, SHARE, 2, 128), F32),
            pltpu.VMEM((2, N_SCEN, 2, 128), F32),
            pltpu.VMEM((N_INST, 2, SHARE, HALF), F32),
            pltpu.VMEM((SHARE, 1, 128), F32),
            pltpu.VMEM((N_INST, SHARE, 1, 128), F32),
            pltpu.VMEM((BOOKS, SCEN_DEV), BF16),
            pltpu.VMEM((CHUNKS, BOOKS // 2, CHUNK), BF16),
            pltpu.VMEM((CHUNKS, BOOKS // 2, CHUNK), BF16),
            pltpu.VMEM((CHUNKS, BOOKS // 2, CHUNK), F32),
            pltpu.VMEM((CHUNKS * 8, SHARE, CHUNK), BF16),
            pltpu.VMEM((CHUNKS * 8, SHARE, CHUNK), BF16),
            dma((N_INST,)),
            dma((5,)),
            dma(()),
            dma((40,)),
            dma((2,)), dma((2,)),
            dma((2,)), dma((2,)),
            dma((2,)), dma((2,)),
            dma((2,)), dma((2,)),
            dma((CHUNKS,)), dma((CHUNKS,)),
            dma((CHUNKS * 8,)), dma((CHUNKS * 8,)),
        ],
        compiler_params=pltpu.CompilerParams(
            collective_id=0, has_side_effects=True, vmem_limit_bytes=60 * 1024 * 1024
        ),
        name="revalue",
    )(
        shocks, loadings, row(delta), row(gamma), row(kappa), row(book_of),
        bracket_low, bracket_high, rank,
    )
    return out, q


def solution(mesh):
    placed = (
        P("scen", "inst"),
        P(None, "inst"),
        P("inst"),
        P("inst"),
        P("inst"),
        P("inst"),
        P(),
        P(),
        P(),
    )
    return jax.shard_map(
        body, mesh=mesh, in_specs=placed, out_specs=(P("scen", "inst"), P("inst")), check_vma=False
    )
```

```python
import functools

import jax
import jax.numpy as jnp
from jax import lax
from jax.experimental import pallas as pl
from jax.experimental.pallas import tpu as pltpu
from jax.sharding import PartitionSpec as P

MESH = pl.DeviceIdType.MESH
F32 = jnp.float32
BF16 = jnp.bfloat16

PIVOTS = 64
ROUNDS = 3
BOOKS = 256
SIDE = 4
N_INST = 16
N_SCEN = 16
RING = 8
SHARE = 16
SCEN_DEV = 512
HALF = 256
FACT_DEV = 128
FACTORS = 2048
INST_DEV = 4096
TILE = 1024
TILES = INST_DEV // TILE
CHUNKS = 4
CHUNK = INST_DEV // CHUNKS
PLACES = (
    (0, 0), (-1, 0), (1, 0), (0, -1), (0, 1),
    (-1, -1), (-1, 1), (1, -1), (1, 1), (2, 0), (0, 2),
    (2, -1), (2, 1), (-1, 2), (1, 2), (2, 2),
)
CUTS = (0, 4, 10, 16)
SCALE = (BOOKS / (INST_DEV * N_INST)) ** 0.5


def sigmoid(v):
    return 1.0 / (1.0 + jnp.exp(-v))


def kernel(
    shocks, loadings, delta, gamma, kappa, book_of, low_in, high_in, rank_in,
    out, qout,
    low, high, rank, LH, LD, ACC, PR, OH, SENS, BK, ST, PS, RS, ROWS, DV, PNL, QR, QA, W,
    SIBS, SIBR, OWNC, RSND, RRCV,
    word, ld_sem, in_sem, a_send, a_recv, c_send, c_recv, d_send, d_recv, g_send, g_recv,
    f_send, f_recv, sib_send, sib_recv, r_send, r_recv,
):
    s = lax.axis_index("scen")
    i = lax.axis_index("inst")
    x, y = lax.div(i, SIDE), lax.rem(i, SIDE)
    z, c = lax.div(s, 2), lax.rem(s, 2)

    def inst_at(dx, dy):
        return lax.rem(x + dx + SIDE, SIDE) * SIDE + lax.rem(y + dy + SIDE, SIDE)

    def inst_peer(k):
        return lax.rem(i + k, N_INST)

    def scen_peer(k):
        return lax.rem(s + k, N_SCEN)

    def ring_pos(d):
        return lax.rem(z + d + RING, RING)

    def remote(src, dst, ssem, rsem, **dev):
        return pltpu.make_async_remote_copy(
            src_ref=src, dst_ref=dst, send_sem=ssem, recv_sem=rsem,
            device_id=dev, device_id_type=MESH,
        )

    def drain(ref, sem):
        pltpu.make_async_copy(ref, ref, sem).wait()

    barrier = pltpu.get_barrier_semaphore()
    for dx, dy in PLACES[1:5]:
        pl.semaphore_signal(barrier, inc=1, device_id={"inst": inst_at(dx, dy)}, device_id_type=MESH)
    up, down, partner = ring_pos(1) * 2 + c, ring_pos(-1) * 2 + c, z * 2 + (1 - c)
    for peer in (partner, up, down):
        pl.semaphore_signal(barrier, inc=1, device_id={"scen": peer}, device_id_type=MESH)

    def tell(r):
        for peer in (up, down):
            pl.semaphore_signal(word.at[r], inc=1, device_id={"scen": peer}, device_id_type=MESH)

    def hear(r):
        pl.semaphore_wait(word.at[r], 2)

    small = [
        pltpu.make_async_copy(shocks, LH.at[:, pl.ds(0, FACT_DEV)], in_sem.at[0]),
        pltpu.make_async_copy(delta, SENS.at[0], in_sem.at[1]),
        pltpu.make_async_copy(gamma, SENS.at[1], in_sem.at[2]),
        pltpu.make_async_copy(kappa, SENS.at[2], in_sem.at[3]),
        pltpu.make_async_copy(book_of, BK, in_sem.at[4]),
        pltpu.make_async_copy(low_in, low, in_sem.at[5]),
        pltpu.make_async_copy(high_in, high, in_sem.at[6]),
        pltpu.make_async_copy(rank_in, rank, in_sem.at[7]),
    ]
    for cp in small:
        cp.start()

    def load_block(p):
        source = inst_at(*PLACES[p])
        return pltpu.make_async_copy(
            loadings.at[pl.ds(pl.multiple_of(source * FACT_DEV, FACT_DEV), FACT_DEV), :],
            LD.at[pl.ds(p * FACT_DEV, FACT_DEV), :],
            ld_sem.at[p],
        )

    for p in range(N_INST):
        load_block(p).start()

    pl.semaphore_wait(barrier, 7)

    def along(colour, first, second):
        return inst_at(first, second) if colour == 0 else inst_at(second, first)

    def place_of(colour, a, b):
        fold = lambda v: (v + 1) % SIDE - 1
        return PLACES.index((fold(a), fold(b)) if colour == 0 else (fold(b), fold(a)))

    def rows_of(colour, part):
        start, size = colour * HALF, HALF
        if part:
            size //= 2
            start += size * (part - 1)
        return pl.ds(start, size)

    def piece(colour, a, b, part):
        return LH.at[rows_of(colour, part), pl.ds(place_of(colour, a, b) * FACT_DEV, FACT_DEV)]

    def a_pass(colour, a, b, part, first, second, pid):
        if (a, b) == (0, 0):
            src = shocks.at[rows_of(colour, part), :]
        else:
            src = piece(colour, a, b, part)
        remote(
            src, piece(colour, a - first, b - second, part), a_send, a_recv.at[colour * 20 + pid],
            inst=along(colour, first, second),
        ).start()

    def a_wait(colour, a, b, part, pid):
        drain(piece(colour, a, b, part), a_recv.at[colour * 20 + pid])

    lanes = (0, -1, 1, 2)

    def a_second(colour, q):
        a_pass(colour, lanes[q], 0, 0, 0, 1, 4 + 4 * q)
        a_pass(colour, lanes[q], 0, 0, 0, -1, 5 + 4 * q)

    def a_hand_on(colour, q):
        a_wait(colour, lanes[q], -1, 0, 4 + 4 * q)
        a_pass(colour, lanes[q], -1, 1, 0, 1, 6 + 4 * q)
        a_wait(colour, lanes[q], 1, 0, 5 + 4 * q)
        a_pass(colour, lanes[q], 1, 2, 0, -1, 7 + 4 * q)

    def a_last(colour, q):
        a_wait(colour, lanes[q], 2, 1, 6 + 4 * q)
        a_wait(colour, lanes[q], 2, 2, 7 + 4 * q)

    def a_step(step):
        for colour in range(2):
            if step == 0:
                a_pass(colour, 0, 0, 0, 1, 0, 0)
                a_pass(colour, 0, 0, 0, -1, 0, 1)
                a_second(colour, 0)
            elif step == 1:
                a_wait(colour, -1, 0, 0, 0)
                a_pass(colour, -1, 0, 1, 1, 0, 2)
                a_second(colour, 1)
                a_wait(colour, 1, 0, 0, 1)
                a_pass(colour, 1, 0, 2, -1, 0, 3)
                a_second(colour, 2)
            elif step == 2:
                a_hand_on(colour, 0)
            elif step == 3:
                a_wait(colour, 2, 0, 1, 2)
                a_wait(colour, 2, 0, 2, 3)
                a_second(colour, 3)
            elif step == 4:
                a_hand_on(colour, 1)
                a_hand_on(colour, 2)
                a_last(colour, 0)
            elif step == 5:
                a_hand_on(colour, 3)
            else:
                for q in range(1, 4):
                    a_last(colour, q)

    a_step(0)
    tell(0)
    small[4].wait()
    book_ids = lax.broadcasted_iota(jnp.int32, (BOOKS, TILE), 0)

    def one_hot(n, carry):
        cols = pl.ds(pl.multiple_of(n * TILE, TILE), TILE)
        OH[cols, :] = jnp.transpose(jnp.where(BK[:, cols] == book_ids, 1.0, 0.0).astype(BF16))
        return carry

    lax.fori_loop(0, TILES, one_hot, 0)
    ST[...] = jnp.zeros_like(ST)
    a_step(1)
    hear(0)
    tell(1)
    a_step(2)
    for cp in small[:4] + small[5:]:
        cp.wait()

    def share_rows(k):
        return pl.ds(pl.multiple_of(k * SHARE, SHARE), SHARE)

    def send_sums(h):
        PS[h] = jnp.transpose(ST[h])

        def one(k, carry):
            p = inst_peer(k)
            remote(PS.at[h, share_rows(p), :], RS.at[h, i], c_send.at[h], c_recv.at[h], inst=p).start()
            return carry

        lax.fori_loop(1, N_INST, one, 0)
        RS[h, i] = PS[h, share_rows(i), :]

    def take_sums(h):
        drain(RS.at[h, pl.ds(0, N_INST - 1)], c_recv.at[h])
        total = RS[h, 0]
        for k in range(1, N_INST):
            total = total + RS[h, k]
        total = total * SCALE
        PNL[i, h] = total
        for r in range(2):
            ROWS[h, :, r, :] = total[:, r * 128 : (r + 1) * 128]

        def one(k, carry):
            p = scen_peer(k)
            remote(ROWS.at[h, p], DV.at[h, s], d_send.at[h], d_recv.at[h], scen=p).start()
            return carry

        lax.fori_loop(1, N_SCEN, one, 0)

        DV[h, s] = ROWS[h, s]

    def share_sums(h):
        def one(k, carry):
            p = inst_peer(k)
            remote(PNL.at[i, h], PNL.at[i, h], g_send.at[h], g_recv.at[h], inst=p).start()
            return carry

        lax.fori_loop(1, N_INST, one, 0)

    def factors(group):
        return pl.ds(CUTS[group] * FACT_DEV, (CUTS[group + 1] - CUTS[group]) * FACT_DEV)

    def wait_blocks(group):
        for p in range(CUTS[group], CUTS[group + 1]):
            load_block(p).wait()

    def tile_cols(n):
        return pl.ds(pl.multiple_of(n * TILE, TILE), TILE)

    def first_group(n, carry):
        cols = tile_cols(n)
        ACC[:, cols] = jnp.dot(LH[:, factors(0)], LD[factors(0), cols], preferred_element_type=F32)
        return carry

    def second_group(n, carry):
        cols = tile_cols(n)
        ACC[:, cols] += jnp.dot(LH[:, factors(1)], LD[factors(1), cols], preferred_element_type=F32)

        @pl.when(n == TILES // 2)
        def _():
            a_step(5)

        return carry

    def last_group(h, n):
        cols = tile_cols(n)
        rows = pl.ds(h * HALF, HALF)
        moves = ACC[rows, cols] + jnp.dot(LH[rows, factors(2)], LD[factors(2), cols], preferred_element_type=F32)
        d, g, k = SENS[0, :, cols], SENS[1, :, cols], SENS[2, :, cols]
        profit = (moves * (d + moves * (g + moves * k))).astype(BF16)
        PR[rows, cols] = profit
        ST[h] += jnp.dot(profit, OH[cols, :], preferred_element_type=F32)

    def last_first(n, carry):
        last_group(0, n)
        return carry

    def last_second(n, carry):
        last_group(1, n)
        return carry

    wait_blocks(0)
    lax.fori_loop(0, TILES, first_group, 0)
    hear(1)
    tell(2)
    a_step(3)
    a_step(4)
    wait_blocks(1)
    lax.fori_loop(0, TILES, second_group, 0)
    hear(2)
    tell(3)
    a_step(6)
    wait_blocks(2)
    hear(3)
    lax.fori_loop(0, TILES, last_first, 0)
    send_sums(0)
    lax.fori_loop(0, TILES, last_second, 0)
    send_sums(1)
    take_sums(0)
    take_sums(1)
    share_sums(0)
    share_sums(1)

    book = i * SHARE + s
    lower = jnp.full((PIVOTS, 128), low[book], jnp.int32).astype(F32) * 0.125
    upper = jnp.full((PIVOTS, 128), high[book], jnp.int32).astype(F32) * 0.125
    wanted = jnp.full((PIVOTS, 128), rank[book], jnp.int32).astype(F32)
    levels = lax.broadcasted_iota(jnp.int32, (PIVOTS, 128), 0).astype(F32)
    for h in range(2):
        drain(DV.at[h, pl.ds(0, N_SCEN - 1)], d_recv.at[h])
    for _ in range(ROUNDS):
        spacing = (upper - lower) / (PIVOTS - 1)
        marks = lower + levels * spacing
        count = jnp.zeros((PIVOTS, 128), F32)
        for h in range(2):
            for p in range(N_SCEN):
                for r in range(2):
                    row = DV[h, p, pl.ds(r, 1), :]
                    count = count + jnp.where(row <= marks, 1.0, 0.0)
        count = jnp.sum(count, axis=1, keepdims=True)
        below = jnp.sum(jnp.where(count < wanted, 1.0, 0.0), axis=0, keepdims=True)
        chosen = jnp.clip(below, 1.0, PIVOTS - 1.0)
        upper = lower + chosen * spacing
        lower = lower + (chosen - 1.0) * spacing
    quantile = (lower + upper) * 0.5
    pair_q = quantile[0:2, :]
    mass = jnp.zeros((2, 128), F32)
    for h in range(2):
        for p in range(N_SCEN):
            mass = mass + sigmoid((pair_q - DV[h, p]) * 2.0).astype(BF16).astype(F32)
    mass = jnp.sum(jnp.sum(mass, axis=1, keepdims=True), axis=0, keepdims=True)
    lane = lax.broadcasted_iota(jnp.int32, (1, 128), 1)
    QR[s] = jnp.where(lane < 64, quantile[0:1, :], jnp.broadcast_to(mass, (1, 128)))

    def send_q(k, carry):
        remote(QR.at[s], QR.at[s], f_send.at[0], f_recv.at[0], scen=scen_peer(k)).start()
        return carry

    lax.fori_loop(1, N_SCEN, send_q, 0)
    drain(QR.at[pl.ds(0, N_SCEN - 1)], f_recv.at[0])

    def send_all_q(k, carry):
        remote(QR, QA.at[i], f_send.at[1], f_recv.at[1], inst=inst_peer(k)).start()
        return carry

    lax.fori_loop(1, N_INST, send_all_q, 0)
    QA[i] = QR[...]
    books = lax.broadcasted_iota(jnp.int32, (SHARE, 128), 0)
    lanes_q = lax.broadcasted_iota(jnp.int32, (SHARE, 128), 1)
    qout[...] = jnp.sum(jnp.where(books == lanes_q, QR[:, 0, :], 0.0), axis=0)[:SHARE]
    for h in range(2):
        drain(PNL.at[pl.ds(0, N_INST - 1), h], g_recv.at[h])
    drain(QA.at[pl.ds(0, N_INST - 1)], f_recv.at[1])

    for t in range(N_INST):
        ahead = lax.rem(t // 2 - z + RING, RING)
        order = jnp.where(ahead == 0, 7, jnp.where(ahead < 4, 7 - 2 * ahead, 2 * ahead - 8))
        place = jnp.where(c == t % 2, BOOKS // 2, 0) + order * SHARE
        q = QA[t, :, 0, :][:, 0:1]
        for h in range(2):
            w = sigmoid((q - PNL[t, h]) * 2.0).astype(BF16)
            W[pl.ds(pl.multiple_of(place, SHARE), SHARE), pl.ds(h * HALF, HALF)] = w

    own_mass = QA[s, :, 0, :][:, 64:65]

    def chunk_cols(n):
        return pl.ds(n * CHUNK, CHUNK)

    def sib_copy(k):
        if k < CHUNKS:
            part = (pl.ds(0, SHARE), chunk_cols(k))
        else:
            start, size = ((1, 2), (3, 2), (5, 3))[k - CHUNKS]
            part = (pl.ds(start * SHARE, size * SHARE), pl.ds(0, INST_DEV))
        return remote(SIBS.at[part], SIBR.at[part], sib_send.at[k], sib_recv.at[k], scen=partner)

    def contribute(n):
        for u in range(2):
            cols = pl.ds(n * CHUNK + u * (CHUNK // 2), CHUNK // 2)
            both = jnp.dot(W[...], PR[:, cols], preferred_element_type=F32)
            SIBS[:, cols] = both[: BOOKS // 2].astype(BF16)
            OWNC[:, cols] = both[BOOKS // 2 :]
        sib_copy(n).start()

    def ring_copy(n, way, step):
        if step == 0:
            cols = pl.ds(way * (CHUNK // 2), CHUNK // 2)
        else:
            cols = pl.ds(0, CHUNK)
        slot = (n * 2 + way) * 4 + step
        return remote(
            RSND.at[slot, :, cols], RRCV.at[slot, :, cols], r_send.at[slot], r_recv.at[slot],
            scen=up if way == 0 else down,
        )

    def held(n, step, way, u, count):
        order = 0 if step == 0 else 7 if step == 4 else 2 * step - 1 + way
        rows = pl.ds(order * SHARE, SHARE)
        cols = pl.ds(n * CHUNK + u * (CHUNK // 2), count * (CHUNK // 2))
        return OWNC[rows, cols] + SIBR[rows, cols].astype(F32)

    def ring_step(n, step):
        halves = (pl.ds(0, CHUNK // 2), pl.ds(CHUNK // 2, CHUNK // 2))
        if step == 4:
            ring_copy(n, 0, 3).wait_recv()
            ring_copy(n, 1, 3).wait_recv()
            total = held(n, 4, 0, 0, 2)
            total = total + RRCV[(n * 2) * 4 + 3].astype(F32) + RRCV[(n * 2 + 1) * 4 + 3].astype(F32)
            out[:, chunk_cols(n)] = total / own_mass
            return
        for way in range(2):
            slot = (n * 2 + way) * 4 + step
            if step == 0:
                RSND[slot, :, halves[way]] = held(n, 0, way, way, 1).astype(BF16)
            else:
                ring_copy(n, way, step - 1).wait_recv()
                for u in range(2):
                    v = held(n, step, way, u, 1)
                    if step > 1 or u == way:
                        v = v + RRCV[slot - 1, :, halves[u]].astype(F32)
                    RSND[slot, :, halves[u]] = v.astype(BF16)
            ring_copy(n, way, step).start()

    for n in range(CHUNKS):
        contribute(n)
    for k in range(CHUNKS, CHUNKS + 3):
        sib_copy(k).start()
    for n in range(CHUNKS):
        sib_copy(n).wait_recv()
        ring_step(n, 0)
    sib_copy(CHUNKS).wait_recv()
    for n in range(CHUNKS):
        ring_step(n, 1)
    sib_copy(CHUNKS + 1).wait_recv()
    for n in range(CHUNKS):
        ring_step(n, 2)
    sib_copy(CHUNKS + 2).wait_recv()
    for n in range(CHUNKS):
        ring_step(n, 3)
    for n in range(CHUNKS):
        ring_step(n, 4)

    drain(LH.at[pl.ds(0, SCEN_DEV * 15 // 16), :], a_send)
    for h in range(2):
        drain(RS.at[h, pl.ds(0, N_INST - 1)], c_send.at[h])
        drain(DV.at[h, pl.ds(0, N_SCEN - 1)], d_send.at[h])
        drain(PNL.at[pl.ds(0, N_INST - 1), h], g_send.at[h])
    drain(QR.at[pl.ds(0, N_SCEN - 1)], f_send.at[0])
    drain(QA.at[pl.ds(0, N_INST - 1)], f_send.at[1])
    for k in range(CHUNKS + 3):
        sib_copy(k).wait_send()
    for n in range(CHUNKS):
        for way in range(2):
            for step in range(4):
                ring_copy(n, way, step).wait_send()


def body(shocks, loadings, delta, gamma, kappa, book_of, bracket_low, bracket_high, rank):
    anywhere = pl.BlockSpec(memory_space=pl.ANY)
    row = lambda v: v.reshape(1, INST_DEV)
    dma = pltpu.SemaphoreType.DMA
    out, q = pl.pallas_call(
        kernel,
        out_shape=(
            pltpu.VMEM((SHARE, INST_DEV), F32),
            pltpu.VMEM((SHARE,), F32),
        ),
        in_specs=[anywhere] * 9,
        out_specs=(pl.BlockSpec(memory_space=pltpu.VMEM),) * 2,
        scratch_shapes=[
            pltpu.SMEM((BOOKS,), jnp.int32),
            pltpu.SMEM((BOOKS,), jnp.int32),
            pltpu.SMEM((BOOKS,), jnp.int32),
            pltpu.VMEM((SCEN_DEV, FACTORS), BF16),
            pltpu.VMEM((FACTORS, INST_DEV), BF16),
            pltpu.VMEM((SCEN_DEV, INST_DEV), F32),
            pltpu.VMEM((SCEN_DEV, INST_DEV), BF16),
            pltpu.VMEM((INST_DEV, BOOKS), BF16),
            pltpu.VMEM((3, 1, INST_DEV), F32),
            pltpu.VMEM((1, INST_DEV), jnp.int32),
            pltpu.VMEM((2, HALF, BOOKS), F32),
            pltpu.VMEM((2, BOOKS, HALF), F32),
            pltpu.VMEM((2, N_INST, SHARE, HALF), F32),
            pltpu.VMEM((2, SHARE, 2, 128), F32),
            pltpu.VMEM((2, N_SCEN, 2, 128), F32),
            pltpu.VMEM((N_INST, 2, SHARE, HALF), F32),
            pltpu.VMEM((SHARE, 1, 128), F32),
            pltpu.VMEM((N_INST, SHARE, 1, 128), F32),
            pltpu.VMEM((BOOKS, SCEN_DEV), BF16),
            pltpu.VMEM((BOOKS // 2, INST_DEV), BF16),
            pltpu.VMEM((BOOKS // 2, INST_DEV), BF16),
            pltpu.VMEM((BOOKS // 2, INST_DEV), F32),
            pltpu.VMEM((CHUNKS * 8, SHARE, CHUNK), BF16),
            pltpu.VMEM((CHUNKS * 8, SHARE, CHUNK), BF16),
            pltpu.SemaphoreType.REGULAR((4,)),
            dma((N_INST,)),
            dma((8,)),
            dma(()),
            dma((40,)),
            dma((2,)), dma((2,)),
            dma((2,)), dma((2,)),
            dma((2,)), dma((2,)),
            dma((2,)), dma((2,)),
            dma((CHUNKS + 3,)), dma((CHUNKS + 3,)),
            dma((CHUNKS * 8,)), dma((CHUNKS * 8,)),
        ],
        compiler_params=pltpu.CompilerParams(
            collective_id=0, has_side_effects=True, vmem_limit_bytes=60 * 1024 * 1024
        ),
        name="revalue",
    )(
        shocks, loadings, row(delta), row(gamma), row(kappa), row(book_of),
        bracket_low, bracket_high, rank,
    )
    return out, q


def solution(mesh):
    placed = (
        P("scen", "inst"),
        P(None, "inst"),
        P("inst"),
        P("inst"),
        P("inst"),
        P("inst"),
        P(),
        P(),
        P(),
    )
    return jax.shard_map(
        body, mesh=mesh, in_specs=placed, out_specs=(P("scen", "inst"), P("inst")), check_vma=False
    )
```

```python
import functools

import jax
import jax.numpy as jnp
from jax import lax
from jax.experimental import pallas as pl
from jax.experimental.pallas import tpu as pltpu
from jax.sharding import PartitionSpec as P

MESH = pl.DeviceIdType.MESH
F32 = jnp.float32
BF16 = jnp.bfloat16

PIVOTS = 64
ROUNDS = 3
BOOKS = 256
SIDE = 4
N_INST = 16
N_SCEN = 16
RING = 8
SHARE = 16
SCEN_DEV = 512
HALF = 256
FACT_DEV = 128
FACTORS = 2048
INST_DEV = 4096
TILE = 1024
TILES = INST_DEV // TILE
CHUNKS = 4
CHUNK = INST_DEV // CHUNKS
PLACES = (
    (0, 0), (-1, 0), (1, 0), (0, -1), (0, 1),
    (-1, -1), (-1, 1), (1, -1), (1, 1), (2, 0), (0, 2),
    (2, -1), (2, 1), (-1, 2), (1, 2), (2, 2),
)
CUTS = (0, 4, 10, 14, 16)
SCALE = (BOOKS / (INST_DEV * N_INST)) ** 0.5


def sigmoid(v):
    return 1.0 / (1.0 + jnp.exp(-v))


def kernel(
    shocks, loadings, delta, gamma, kappa, book_of, low_in, high_in, rank_in,
    out, qout,
    low, high, rank, LH, LD, ACC, PR, OH, SENS, BK, ST, PS, RS, ROWS, DV, PNL, QR, QA, W,
    SIBS, SIBR, OWNC, RSND, RRCV,
    word, ld_sem, in_sem, a_send, a_recv, c_send, c_recv, d_send, d_recv, g_send, g_recv,
    f_send, f_recv, sib_send, sib_recv, r_send, r_recv,
):
    s = lax.axis_index("scen")
    i = lax.axis_index("inst")
    x, y = lax.div(i, SIDE), lax.rem(i, SIDE)
    z, c = lax.div(s, 2), lax.rem(s, 2)

    def inst_at(dx, dy):
        return lax.rem(x + dx + SIDE, SIDE) * SIDE + lax.rem(y + dy + SIDE, SIDE)

    def inst_peers():
        return [inst_at(dx, dy) for dx, dy in PLACES[:0:-1]]

    def scen_peers():
        return [lax.rem(s + k, N_SCEN) for k in sorted(range(1, N_SCEN), key=lambda k: abs(k - N_SCEN // 2))]

    def ring_pos(d):
        return lax.rem(z + d + RING, RING)

    def remote(src, dst, ssem, rsem, **dev):
        return pltpu.make_async_remote_copy(
            src_ref=src, dst_ref=dst, send_sem=ssem, recv_sem=rsem,
            device_id=dev, device_id_type=MESH,
        )

    def drain(ref, sem):
        pltpu.make_async_copy(ref, ref, sem).wait()

    barrier = pltpu.get_barrier_semaphore()
    for dx, dy in PLACES[1:5]:
        pl.semaphore_signal(barrier, inc=1, device_id={"inst": inst_at(dx, dy)}, device_id_type=MESH)
    up, down, partner = ring_pos(1) * 2 + c, ring_pos(-1) * 2 + c, z * 2 + (1 - c)
    for peer in (partner, up, down):
        pl.semaphore_signal(barrier, inc=1, device_id={"scen": peer}, device_id_type=MESH)

    def tell(r):
        for peer in (up, down):
            pl.semaphore_signal(word.at[r], inc=1, device_id={"scen": peer}, device_id_type=MESH)

    def hear(r):
        pl.semaphore_wait(word.at[r], 2)

    small = [
        pltpu.make_async_copy(shocks, LH.at[0], in_sem.at[0]),
        pltpu.make_async_copy(delta, SENS.at[0], in_sem.at[1]),
        pltpu.make_async_copy(gamma, SENS.at[1], in_sem.at[2]),
        pltpu.make_async_copy(kappa, SENS.at[2], in_sem.at[3]),
        pltpu.make_async_copy(book_of, BK, in_sem.at[4]),
        pltpu.make_async_copy(low_in, low, in_sem.at[5]),
        pltpu.make_async_copy(high_in, high, in_sem.at[6]),
        pltpu.make_async_copy(rank_in, rank, in_sem.at[7]),
    ]
    for cp in small:
        cp.start()

    def load_block(p):
        source = inst_at(*PLACES[p])
        return pltpu.make_async_copy(
            loadings.at[pl.ds(pl.multiple_of(source * FACT_DEV, FACT_DEV), FACT_DEV), :],
            LD.at[pl.ds(p * FACT_DEV, FACT_DEV), :],
            ld_sem.at[p],
        )

    def start_blocks(group):
        for p in range(CUTS[group], CUTS[group + 1]):
            load_block(p).start()

    start_blocks(0)

    pl.semaphore_wait(barrier, 7)

    def along(colour, first, second):
        return inst_at(first, second) if colour == 0 else inst_at(second, first)

    def place_of(colour, a, b):
        fold = lambda v: (v + 1) % SIDE - 1
        return PLACES.index((fold(a), fold(b)) if colour == 0 else (fold(b), fold(a)))

    def rows_of(colour, h, part):
        size = HALF // 2
        start = colour * HALF + h * size
        if part:
            size //= 2
            start += size * (part - 1)
        return pl.ds(start, size)

    def piece(colour, h, a, b, part):
        return LH.at[place_of(colour, a, b), rows_of(colour, h, part), :]

    def a_pass(colour, h, a, b, part, first, second, pid):
        if (a, b) == (0, 0):
            src = shocks.at[rows_of(colour, h, part), :]
        else:
            src = piece(colour, h, a, b, part)
        remote(
            src, piece(colour, h, a - first, b - second, part), a_send, a_recv.at[(h * 2 + colour) * 20 + pid],
            inst=along(colour, first, second),
        ).start()

    def a_wait(colour, h, a, b, part, pid):
        drain(piece(colour, h, a, b, part), a_recv.at[(h * 2 + colour) * 20 + pid])

    lanes = (0, -1, 1, 2)

    def a_second(colour, h, q):
        a_pass(colour, h, lanes[q], 0, 0, 0, 1, 4 + 4 * q)
        a_pass(colour, h, lanes[q], 0, 0, 0, -1, 5 + 4 * q)

    def a_hand_on(colour, h, q):
        a_wait(colour, h, lanes[q], -1, 0, 4 + 4 * q)
        a_pass(colour, h, lanes[q], -1, 1, 0, 1, 6 + 4 * q)
        a_wait(colour, h, lanes[q], 1, 0, 5 + 4 * q)
        a_pass(colour, h, lanes[q], 1, 2, 0, -1, 7 + 4 * q)

    def a_last(colour, h, q):
        a_wait(colour, h, lanes[q], 2, 1, 6 + 4 * q)
        a_wait(colour, h, lanes[q], 2, 2, 7 + 4 * q)

    def a_step(h, step):
        for colour in range(2):
            if step == 0:
                a_pass(colour, h, 0, 0, 0, 1, 0, 0)
                a_pass(colour, h, 0, 0, 0, -1, 0, 1)
                a_second(colour, h, 0)
            elif step == 1:
                a_wait(colour, h, -1, 0, 0, 0)
                a_pass(colour, h, -1, 0, 1, 1, 0, 2)
                a_second(colour, h, 1)
                a_wait(colour, h, 1, 0, 0, 1)
                a_pass(colour, h, 1, 0, 2, -1, 0, 3)
                a_second(colour, h, 2)
            elif step == 2:
                a_hand_on(colour, h, 0)
            elif step == 3:
                a_wait(colour, h, 2, 0, 1, 2)
                a_wait(colour, h, 2, 0, 2, 3)
                a_second(colour, h, 3)
            elif step == 4:
                a_hand_on(colour, h, 1)
                a_hand_on(colour, h, 2)
                a_last(colour, h, 0)
            elif step == 5:
                a_hand_on(colour, h, 3)
            elif step == 6:
                a_last(colour, h, 1)
                a_last(colour, h, 2)
            else:
                a_last(colour, h, 3)

    a_step(0, 0)
    a_step(1, 0)
    tell(0)
    small[4].wait()
    book_ids = lax.broadcasted_iota(jnp.int32, (BOOKS, TILE), 0)

    def one_hot(n, carry):
        cols = pl.ds(pl.multiple_of(n * TILE, TILE), TILE)
        OH[cols, :] = jnp.transpose(jnp.where(BK[:, cols] == book_ids, 1.0, 0.0).astype(BF16))
        return carry

    lax.fori_loop(0, TILES, one_hot, 0)
    start_blocks(1)
    ST[...] = jnp.zeros_like(ST)
    a_step(0, 1)
    a_step(0, 2)
    a_step(1, 1)
    a_step(1, 2)
    start_blocks(2)
    start_blocks(3)
    hear(0)
    tell(1)
    for cp in small[:4] + small[5:]:
        cp.wait()

    def share_rows(k):
        return pl.ds(pl.multiple_of(k * SHARE, SHARE), SHARE)

    def send_sums(h):
        PS[h] = jnp.transpose(ST[h])

        for p in inst_peers():
            remote(PS.at[h, share_rows(p), :], RS.at[h, i], c_send.at[h], c_recv.at[h], inst=p).start()
        RS[h, i] = PS[h, share_rows(i), :]

    def take_sums(h):
        drain(RS.at[h, pl.ds(0, N_INST - 1)], c_recv.at[h])
        total = RS[h, 0]
        for k in range(1, N_INST):
            total = total + RS[h, k]
        total = total * SCALE
        PNL[i, h] = total
        for r in range(2):
            ROWS[h, :, r, :] = total[:, r * 128 : (r + 1) * 128]

        for p in scen_peers():
            remote(ROWS.at[h, p], DV.at[h, s], d_send.at[h], d_recv.at[h], scen=p).start()

        DV[h, s] = ROWS[h, s]

    def share_sums(h):
        for p in inst_peers():
            remote(PNL.at[i, h], PNL.at[i, h], g_send.at[h], g_recv.at[h], inst=p).start()

    def factors(group):
        return pl.ds(CUTS[group] * FACT_DEV, (CUTS[group + 1] - CUTS[group]) * FACT_DEV)

    def scenarios(group, rows):
        return jnp.concatenate([LH[p, rows, :] for p in range(CUTS[group], CUTS[group + 1])], axis=1)

    def wait_blocks(group):
        for p in range(CUTS[group], CUTS[group + 1]):
            load_block(p).wait()

    def tile_cols(n):
        return pl.ds(pl.multiple_of(n * TILE, TILE), TILE)

    def first_group(n, carry):
        cols = tile_cols(n)
        ACC[:, cols] = jnp.dot(scenarios(0, slice(None)), LD[factors(0), cols], preferred_element_type=F32)

        @pl.when(n == TILES - 1)
        def _():
            a_step(0, 3)
            a_step(0, 4)

        return carry

    def second_group(n, carry):
        cols = tile_cols(n)
        ACC[:, cols] += jnp.dot(scenarios(1, slice(None)), LD[factors(1), cols], preferred_element_type=F32)

        for h in range(2):
            @pl.when(n == TILES // 2 + h)
            def _():
                a_step(h, 5)

        return carry

    def third_group(n, carry):
        cols = tile_cols(n)
        ACC[:, cols] += jnp.dot(scenarios(2, slice(None)), LD[factors(2), cols], preferred_element_type=F32)
        return carry

    def last_group(h, n):
        cols = tile_cols(n)
        rows = pl.ds(h * HALF, HALF)
        moves = ACC[rows, cols] + jnp.dot(scenarios(3, rows), LD[factors(3), cols], preferred_element_type=F32)
        d, g, k = SENS[0, :, cols], SENS[1, :, cols], SENS[2, :, cols]
        profit = (moves * (d + moves * (g + moves * k))).astype(BF16)
        PR[rows, cols] = profit
        ST[h] += jnp.dot(profit, OH[cols, :], preferred_element_type=F32)

    def last_first(n, carry):
        last_group(0, n)
        return carry

    def last_second(n, carry):
        last_group(1, n)
        return carry

    wait_blocks(0)
    lax.fori_loop(0, TILES, first_group, 0)
    hear(1)
    tell(2)
    a_step(1, 3)
    a_step(1, 4)
    wait_blocks(1)
    lax.fori_loop(0, TILES, second_group, 0)
    hear(2)
    tell(3)
    for h in range(2):
        a_step(h, 6)
    wait_blocks(2)
    lax.fori_loop(0, TILES, third_group, 0)
    for h in range(2):
        a_step(h, 7)
    wait_blocks(3)
    hear(3)
    lax.fori_loop(0, TILES, last_first, 0)
    send_sums(0)
    lax.fori_loop(0, TILES, last_second, 0)
    send_sums(1)
    take_sums(0)
    take_sums(1)
    share_sums(0)
    share_sums(1)

    book = i * SHARE + s
    lower = jnp.full((PIVOTS, 128), low[book], jnp.int32).astype(F32) * 0.125
    upper = jnp.full((PIVOTS, 128), high[book], jnp.int32).astype(F32) * 0.125
    wanted = jnp.full((PIVOTS, 128), rank[book], jnp.int32).astype(F32)
    levels = lax.broadcasted_iota(jnp.int32, (PIVOTS, 128), 0).astype(F32)
    for h in range(2):
        drain(DV.at[h, pl.ds(0, N_SCEN - 1)], d_recv.at[h])
    for _ in range(ROUNDS):
        spacing = (upper - lower) / (PIVOTS - 1)
        marks = lower + levels * spacing
        count = jnp.zeros((PIVOTS, 128), F32)
        for h in range(2):
            for p in range(N_SCEN):
                for r in range(2):
                    row = DV[h, p, pl.ds(r, 1), :]
                    count = count + jnp.where(row <= marks, 1.0, 0.0)
        count = jnp.sum(count, axis=1, keepdims=True)
        below = jnp.sum(jnp.where(count < wanted, 1.0, 0.0), axis=0, keepdims=True)
        chosen = jnp.clip(below, 1.0, PIVOTS - 1.0)
        upper = lower + chosen * spacing
        lower = lower + (chosen - 1.0) * spacing
    quantile = (lower + upper) * 0.5
    pair_q = quantile[0:2, :]
    mass = jnp.zeros((2, 128), F32)
    for h in range(2):
        for p in range(N_SCEN):
            mass = mass + sigmoid((pair_q - DV[h, p]) * 2.0).astype(BF16).astype(F32)
    mass = jnp.sum(jnp.sum(mass, axis=1, keepdims=True), axis=0, keepdims=True)
    lane = lax.broadcasted_iota(jnp.int32, (1, 128), 1)
    QR[s] = jnp.where(lane < 64, quantile[0:1, :], jnp.broadcast_to(mass, (1, 128)))

    for p in scen_peers():
        remote(QR.at[s], QR.at[s], f_send.at[0], f_recv.at[0], scen=p).start()
    drain(QR.at[pl.ds(0, N_SCEN - 1)], f_recv.at[0])

    line = lax.broadcasted_iota(jnp.int32, (SHARE, 128), 0)
    lane = lax.broadcasted_iota(jnp.int32, (SHARE, 128), 1)
    at_q, at_mass = lane == line, lane == line + 64
    row_q = jnp.sum(jnp.where(at_q | at_mass, QR[:, 0, :], 0.0), axis=0, keepdims=True)
    QA[i] = row_q
    for p in inst_peers():
        remote(QA.at[i], QA.at[i], f_send.at[1], f_recv.at[1], inst=p).start()
    qout[...] = row_q[0, :SHARE]

    def column(t, where):
        return jnp.sum(jnp.where(where, jnp.broadcast_to(QA[t], (SHARE, 128)), 0.0), axis=1, keepdims=True)

    for h in range(2):
        drain(PNL.at[pl.ds(0, N_INST - 1), h], g_recv.at[h])
    drain(QA.at[pl.ds(0, N_INST - 1)], f_recv.at[1])

    for t in range(N_INST):
        ahead = lax.rem(t // 2 - z + RING, RING)
        order = jnp.where(ahead == 0, 7, jnp.where(ahead < 4, 7 - 2 * ahead, 2 * ahead - 8))
        place = jnp.where(c == t % 2, BOOKS // 2, 0) + order * SHARE
        q = column(t, at_q)
        for h in range(2):
            w = sigmoid((q - PNL[t, h]) * 2.0).astype(BF16)
            W[pl.ds(pl.multiple_of(place, SHARE), SHARE), pl.ds(h * HALF, HALF)] = w

    own_mass = column(s, at_mass)

    def chunk_cols(n):
        return pl.ds(n * CHUNK, CHUNK)

    def sib_copy(k):
        if k < CHUNKS:
            part = (pl.ds(0, SHARE), chunk_cols(k))
        elif k < 2 * CHUNKS:
            part = (pl.ds(SHARE, 2 * SHARE), chunk_cols(k - CHUNKS))
        else:
            start, size = ((3, 2), (5, 3))[k - 2 * CHUNKS]
            part = (pl.ds(start * SHARE, size * SHARE), pl.ds(0, INST_DEV))
        return remote(SIBS.at[part], SIBR.at[part], sib_send.at[k], sib_recv.at[k], scen=partner)

    def contribute(n):
        for u in range(2):
            cols = pl.ds(n * CHUNK + u * (CHUNK // 2), CHUNK // 2)
            both = jnp.dot(W[...], PR[:, cols], preferred_element_type=F32)
            SIBS[:, cols] = both[: BOOKS // 2].astype(BF16)
            OWNC[:, cols] = both[BOOKS // 2 :]
        sib_copy(n).start()
        sib_copy(CHUNKS + n).start()

    def ring_copy(n, way, step):
        if step == 0:
            cols = pl.ds(way * (CHUNK // 2), CHUNK // 2)
        else:
            cols = pl.ds(0, CHUNK)
        slot = (n * 2 + way) * 4 + step
        return remote(
            RSND.at[slot, :, cols], RRCV.at[slot, :, cols], r_send.at[slot], r_recv.at[slot],
            scen=up if way == 0 else down,
        )

    def held(n, step, way, u, count):
        order = 0 if step == 0 else 7 if step == 4 else 2 * step - 1 + way
        rows = pl.ds(order * SHARE, SHARE)
        cols = pl.ds(n * CHUNK + u * (CHUNK // 2), count * (CHUNK // 2))
        return OWNC[rows, cols] + SIBR[rows, cols].astype(F32)

    def ring_step(n, step):
        halves = (pl.ds(0, CHUNK // 2), pl.ds(CHUNK // 2, CHUNK // 2))
        if step == 4:
            ring_copy(n, 0, 3).wait_recv()
            ring_copy(n, 1, 3).wait_recv()
            total = held(n, 4, 0, 0, 2)
            total = total + RRCV[(n * 2) * 4 + 3].astype(F32) + RRCV[(n * 2 + 1) * 4 + 3].astype(F32)
            out[:, chunk_cols(n)] = total / own_mass
            return
        for way in range(2):
            slot = (n * 2 + way) * 4 + step
            if step == 0:
                RSND[slot, :, halves[way]] = held(n, 0, way, way, 1).astype(BF16)
            else:
                ring_copy(n, way, step - 1).wait_recv()
                for u in range(2):
                    v = held(n, step, way, u, 1)
                    if step > 1 or u == way:
                        v = v + RRCV[slot - 1, :, halves[u]].astype(F32)
                    RSND[slot, :, halves[u]] = v.astype(BF16)
            ring_copy(n, way, step).start()

    def first_step(n):
        sib_copy(n).wait_recv()
        ring_step(n, 0)

    for n in range(CHUNKS):
        contribute(n)
    for k in range(2):
        sib_copy(2 * CHUNKS + k).start()
    for n in range(CHUNKS):
        first_step(n)
    for n in range(CHUNKS):
        sib_copy(CHUNKS + n).wait_recv()
        ring_step(n, 1)
    sib_copy(2 * CHUNKS).wait_recv()
    for n in range(CHUNKS):
        ring_step(n, 2)
    sib_copy(2 * CHUNKS + 1).wait_recv()
    for n in range(CHUNKS):
        ring_step(n, 3)
    for n in range(CHUNKS):
        ring_step(n, 4)

    drain(LH.at[pl.ds(0, N_INST - 1)], a_send)
    for h in range(2):
        drain(RS.at[h, pl.ds(0, N_INST - 1)], c_send.at[h])
        drain(DV.at[h, pl.ds(0, N_SCEN - 1)], d_send.at[h])
        drain(PNL.at[pl.ds(0, N_INST - 1), h], g_send.at[h])
    drain(QR.at[pl.ds(0, N_SCEN - 1)], f_send.at[0])
    drain(QA.at[pl.ds(0, N_INST - 1)], f_send.at[1])
    for k in range(2 * CHUNKS + 2):
        sib_copy(k).wait_send()
    for n in range(CHUNKS):
        for way in range(2):
            for step in range(4):
                ring_copy(n, way, step).wait_send()


def body(shocks, loadings, delta, gamma, kappa, book_of, bracket_low, bracket_high, rank):
    anywhere = pl.BlockSpec(memory_space=pl.ANY)
    row = lambda v: v.reshape(1, INST_DEV)
    dma = pltpu.SemaphoreType.DMA
    out, q = pl.pallas_call(
        kernel,
        out_shape=(
            pltpu.VMEM((SHARE, INST_DEV), F32),
            pltpu.VMEM((SHARE,), F32),
        ),
        in_specs=[anywhere] * 9,
        out_specs=(pl.BlockSpec(memory_space=pltpu.VMEM),) * 2,
        scratch_shapes=[
            pltpu.SMEM((BOOKS,), jnp.int32),
            pltpu.SMEM((BOOKS,), jnp.int32),
            pltpu.SMEM((BOOKS,), jnp.int32),
            pltpu.VMEM((N_INST, SCEN_DEV, FACT_DEV), BF16),
            pltpu.VMEM((FACTORS, INST_DEV), BF16),
            pltpu.VMEM((SCEN_DEV, INST_DEV), F32),
            pltpu.VMEM((SCEN_DEV, INST_DEV), BF16),
            pltpu.VMEM((INST_DEV, BOOKS), BF16),
            pltpu.VMEM((3, 1, INST_DEV), F32),
            pltpu.VMEM((1, INST_DEV), jnp.int32),
            pltpu.VMEM((2, HALF, BOOKS), F32),
            pltpu.VMEM((2, BOOKS, HALF), F32),
            pltpu.VMEM((2, N_INST, SHARE, HALF), F32),
            pltpu.VMEM((2, SHARE, 2, 128), F32),
            pltpu.VMEM((2, N_SCEN, 2, 128), F32),
            pltpu.VMEM((N_INST, 2, SHARE, HALF), F32),
            pltpu.VMEM((SHARE, 1, 128), F32),
            pltpu.VMEM((N_INST, 1, 128), F32),
            pltpu.VMEM((BOOKS, SCEN_DEV), BF16),
            pltpu.VMEM((BOOKS // 2, INST_DEV), BF16),
            pltpu.VMEM((BOOKS // 2, INST_DEV), BF16),
            pltpu.VMEM((BOOKS // 2, INST_DEV), F32),
            pltpu.VMEM((CHUNKS * 8, SHARE, CHUNK), BF16),
            pltpu.VMEM((CHUNKS * 8, SHARE, CHUNK), BF16),
            pltpu.SemaphoreType.REGULAR((4,)),
            dma((N_INST,)),
            dma((8,)),
            dma(()),
            dma((80,)),
            dma((2,)), dma((2,)),
            dma((2,)), dma((2,)),
            dma((2,)), dma((2,)),
            dma((2,)), dma((2,)),
            dma((2 * CHUNKS + 2,)), dma((2 * CHUNKS + 2,)),
            dma((CHUNKS * 8,)), dma((CHUNKS * 8,)),
        ],
        compiler_params=pltpu.CompilerParams(
            collective_id=0, has_side_effects=True, vmem_limit_bytes=60 * 1024 * 1024
        ),
        name="revalue",
    )(
        shocks, loadings, row(delta), row(gamma), row(kappa), row(book_of),
        bracket_low, bracket_high, rank,
    )
    return out, q


def solution(mesh):
    placed = (
        P("scen", "inst"),
        P(None, "inst"),
        P("inst"),
        P("inst"),
        P("inst"),
        P("inst"),
        P(),
        P(),
        P(),
    )
    return jax.shard_map(
        body, mesh=mesh, in_specs=placed, out_specs=(P("scen", "inst"), P("inst")), check_vma=False
    )
```

```python
import functools

import jax
import jax.numpy as jnp
from jax import lax
from jax.experimental import pallas as pl
from jax.experimental.pallas import tpu as pltpu
from jax.sharding import PartitionSpec as P

MESH = pl.DeviceIdType.MESH
F32 = jnp.float32
BF16 = jnp.bfloat16

PIVOTS = 64
ROUNDS = 3
BOOKS = 256
SIDE = 4
N_INST = 16
N_SCEN = 16
RING = 8
SHARE = 16
SCEN_DEV = 512
HALF = 256
FACT_DEV = 128
FACTORS = 2048
INST_DEV = 4096
TILE = 2048
TILES = INST_DEV // TILE
CHUNKS = 4
CHUNK = INST_DEV // CHUNKS
PLACES = (
    (0, 0), (-1, 0), (1, 0), (0, -1), (0, 1),
    (-1, -1), (-1, 1), (1, -1), (1, 1), (2, 0), (0, 2),
    (2, -1), (2, 1), (-1, 2), (1, 2), (2, 2),
)
CUTS = (0, 4, 10, 14, 16)
SCALE = (BOOKS / (INST_DEV * N_INST)) ** 0.5


def sigmoid(v):
    return 1.0 / (1.0 + jnp.exp(-v))


def kernel(
    shocks, loadings, delta, gamma, kappa, book_of, low_in, high_in, rank_in,
    out, qout,
    low, high, rank, LH, LD, ACC, PR, OH, SENS, BK, ST, PS, RS, ROWS, DV, PNL, QR, QA, W,
    SIBS, SIBR, OWNC, RSND, RRCV,
    word, ld_sem, in_sem, a_send, a_recv, c_send, c_recv, d_send, d_recv, g_send, g_recv,
    f_send, f_recv, sib_send, sib_recv, r_send, r_recv,
):
    s = lax.axis_index("scen")
    i = lax.axis_index("inst")
    x, y = lax.div(i, SIDE), lax.rem(i, SIDE)
    z, c = lax.div(s, 2), lax.rem(s, 2)

    def inst_at(dx, dy):
        return lax.rem(x + dx + SIDE, SIDE) * SIDE + lax.rem(y + dy + SIDE, SIDE)

    def inst_peers():
        return [inst_at(dx, dy) for dx, dy in PLACES[:0:-1]]

    def scen_peers():
        return [lax.rem(s + k, N_SCEN) for k in sorted(range(1, N_SCEN), key=lambda k: abs(k - N_SCEN // 2))]

    def ring_pos(d):
        return lax.rem(z + d + RING, RING)

    def remote(src, dst, ssem, rsem, **dev):
        return pltpu.make_async_remote_copy(
            src_ref=src, dst_ref=dst, send_sem=ssem, recv_sem=rsem,
            device_id=dev, device_id_type=MESH,
        )

    def drain(ref, sem):
        pltpu.make_async_copy(ref, ref, sem).wait()

    barrier = pltpu.get_barrier_semaphore()
    for dx, dy in PLACES[1:5]:
        pl.semaphore_signal(barrier, inc=1, device_id={"inst": inst_at(dx, dy)}, device_id_type=MESH)
    up, down, partner = ring_pos(1) * 2 + c, ring_pos(-1) * 2 + c, z * 2 + (1 - c)
    for peer in (partner, up, down):
        pl.semaphore_signal(barrier, inc=1, device_id={"scen": peer}, device_id_type=MESH)

    def tell(r):
        for peer in (up, down):
            pl.semaphore_signal(word.at[r], inc=1, device_id={"scen": peer}, device_id_type=MESH)

    def hear(r):
        pl.semaphore_wait(word.at[r], 2)

    small = [
        pltpu.make_async_copy(shocks, LH.at[0], in_sem.at[0]),
        pltpu.make_async_copy(delta, SENS.at[0], in_sem.at[1]),
        pltpu.make_async_copy(gamma, SENS.at[1], in_sem.at[2]),
        pltpu.make_async_copy(kappa, SENS.at[2], in_sem.at[3]),
        pltpu.make_async_copy(book_of, BK, in_sem.at[4]),
        pltpu.make_async_copy(low_in, low, in_sem.at[5]),
        pltpu.make_async_copy(high_in, high, in_sem.at[6]),
        pltpu.make_async_copy(rank_in, rank, in_sem.at[7]),
    ]
    for cp in small:
        cp.start()

    def load_block(p):
        source = inst_at(*PLACES[p])
        return pltpu.make_async_copy(
            loadings.at[pl.ds(pl.multiple_of(source * FACT_DEV, FACT_DEV), FACT_DEV), :],
            LD.at[pl.ds(p * FACT_DEV, FACT_DEV), :],
            ld_sem.at[p],
        )

    def start_blocks(group):
        for p in range(CUTS[group], CUTS[group + 1]):
            load_block(p).start()

    start_blocks(0)

    pl.semaphore_wait(barrier, 7)

    def along(colour, first, second):
        return inst_at(first, second) if colour == 0 else inst_at(second, first)

    def place_of(colour, a, b):
        fold = lambda v: (v + 1) % SIDE - 1
        return PLACES.index((fold(a), fold(b)) if colour == 0 else (fold(b), fold(a)))

    def rows_of(colour, h, part):
        size = HALF // 2
        start = colour * HALF + h * size
        if part:
            size //= 2
            start += size * (part - 1)
        return pl.ds(start, size)

    def piece(colour, h, a, b, part):
        return LH.at[place_of(colour, a, b), rows_of(colour, h, part), :]

    def a_pass(colour, h, a, b, part, first, second, pid):
        if (a, b) == (0, 0):
            src = shocks.at[rows_of(colour, h, part), :]
        else:
            src = piece(colour, h, a, b, part)
        remote(
            src, piece(colour, h, a - first, b - second, part), a_send, a_recv.at[(h * 2 + colour) * 20 + pid],
            inst=along(colour, first, second),
        ).start()

    def a_wait(colour, h, a, b, part, pid):
        drain(piece(colour, h, a, b, part), a_recv.at[(h * 2 + colour) * 20 + pid])

    lanes = (0, -1, 1, 2)

    def a_second(colour, h, q):
        a_pass(colour, h, lanes[q], 0, 0, 0, 1, 4 + 4 * q)
        a_pass(colour, h, lanes[q], 0, 0, 0, -1, 5 + 4 * q)

    def a_hand_on(colour, h, q):
        a_wait(colour, h, lanes[q], -1, 0, 4 + 4 * q)
        a_pass(colour, h, lanes[q], -1, 1, 0, 1, 6 + 4 * q)
        a_wait(colour, h, lanes[q], 1, 0, 5 + 4 * q)
        a_pass(colour, h, lanes[q], 1, 2, 0, -1, 7 + 4 * q)

    def a_last(colour, h, q):
        a_wait(colour, h, lanes[q], 2, 1, 6 + 4 * q)
        a_wait(colour, h, lanes[q], 2, 2, 7 + 4 * q)

    def a_step(h, step):
        for colour in range(2):
            if step == 0:
                a_pass(colour, h, 0, 0, 0, 1, 0, 0)
                a_pass(colour, h, 0, 0, 0, -1, 0, 1)
                a_second(colour, h, 0)
            elif step == 1:
                a_wait(colour, h, -1, 0, 0, 0)
                a_pass(colour, h, -1, 0, 1, 1, 0, 2)
                a_second(colour, h, 1)
                a_wait(colour, h, 1, 0, 0, 1)
                a_pass(colour, h, 1, 0, 2, -1, 0, 3)
                a_second(colour, h, 2)
            elif step == 2:
                a_hand_on(colour, h, 0)
            elif step == 3:
                a_wait(colour, h, 2, 0, 1, 2)
                a_wait(colour, h, 2, 0, 2, 3)
                a_second(colour, h, 3)
            elif step == 4:
                a_hand_on(colour, h, 1)
                a_hand_on(colour, h, 2)
                a_last(colour, h, 0)
            elif step == 5:
                a_hand_on(colour, h, 3)
            elif step == 6:
                a_last(colour, h, 1)
                a_last(colour, h, 2)
            else:
                a_last(colour, h, 3)

    a_step(0, 0)
    a_step(1, 0)
    tell(0)
    small[4].wait()
    book_ids = lax.broadcasted_iota(jnp.int32, (BOOKS, TILE), 0)

    def one_hot(n, carry):
        cols = pl.ds(pl.multiple_of(n * TILE, TILE), TILE)
        OH[cols, :] = jnp.transpose(jnp.where(BK[:, cols] == book_ids, 1.0, 0.0).astype(BF16))
        return carry

    lax.fori_loop(0, TILES, one_hot, 0)
    start_blocks(1)
    ST[...] = jnp.zeros_like(ST)
    a_step(0, 1)
    a_step(0, 2)
    a_step(1, 1)
    a_step(1, 2)
    start_blocks(2)
    start_blocks(3)
    hear(0)
    tell(1)
    for cp in small[:4] + small[5:]:
        cp.wait()

    def share_rows(k):
        return pl.ds(pl.multiple_of(k * SHARE, SHARE), SHARE)

    def send_sums(h):
        PS[h] = jnp.transpose(ST[h])

        for p in inst_peers():
            remote(PS.at[h, share_rows(p), :], RS.at[h, i], c_send.at[h], c_recv.at[h], inst=p).start()
        RS[h, i] = PS[h, share_rows(i), :]

    def take_sums(h):
        drain(RS.at[h, pl.ds(0, N_INST - 1)], c_recv.at[h])
        total = RS[h, 0]
        for k in range(1, N_INST):
            total = total + RS[h, k]
        total = total * SCALE
        PNL[i, h] = total
        for r in range(2):
            ROWS[h, :, r, :] = total[:, r * 128 : (r + 1) * 128]

        for p in scen_peers():
            remote(ROWS.at[h, p], DV.at[h, s], d_send.at[h], d_recv.at[h], scen=p).start()

        DV[h, s] = ROWS[h, s]

    def share_sums(h):
        for p in inst_peers():
            remote(PNL.at[i, h], PNL.at[i, h], g_send.at[h], g_recv.at[h], inst=p).start()

    def factors(group):
        return pl.ds(CUTS[group] * FACT_DEV, (CUTS[group + 1] - CUTS[group]) * FACT_DEV)

    def scenarios(group, rows):
        return jnp.concatenate([LH[p, rows, :] for p in range(CUTS[group], CUTS[group + 1])], axis=1)

    def wait_blocks(group):
        for p in range(CUTS[group], CUTS[group + 1]):
            load_block(p).wait()

    def tile_cols(n):
        return pl.ds(pl.multiple_of(n * TILE, TILE), TILE)

    def first_group(n, carry):
        cols = tile_cols(n)
        ACC[:, cols] = jnp.dot(scenarios(0, slice(None)), LD[factors(0), cols], preferred_element_type=F32)

        @pl.when(n == TILES - 1)
        def _():
            a_step(0, 3)
            a_step(0, 4)

        return carry

    def second_group(n, carry):
        cols = tile_cols(n)
        ACC[:, cols] += jnp.dot(scenarios(1, slice(None)), LD[factors(1), cols], preferred_element_type=F32)

        @pl.when(n == TILES - 1)
        def _():
            a_step(0, 5)
            a_step(1, 5)

        return carry

    def third_group(n, carry):
        cols = tile_cols(n)
        ACC[:, cols] += jnp.dot(scenarios(2, slice(None)), LD[factors(2), cols], preferred_element_type=F32)
        return carry

    def last_group(h, n):
        cols = tile_cols(n)
        rows = pl.ds(h * HALF, HALF)
        moves = ACC[rows, cols] + jnp.dot(scenarios(3, rows), LD[factors(3), cols], preferred_element_type=F32)
        d, g, k = SENS[0, :, cols], SENS[1, :, cols], SENS[2, :, cols]
        profit = (moves * (d + moves * (g + moves * k))).astype(BF16)
        PR[rows, cols] = profit
        ST[h] += jnp.dot(profit, OH[cols, :], preferred_element_type=F32)

    def last_first(n, carry):
        last_group(0, n)
        return carry

    def last_second(n, carry):
        last_group(1, n)
        return carry

    wait_blocks(0)
    lax.fori_loop(0, TILES, first_group, 0)
    hear(1)
    tell(2)
    a_step(1, 3)
    a_step(1, 4)
    wait_blocks(1)
    lax.fori_loop(0, TILES, second_group, 0)
    hear(2)
    tell(3)
    for h in range(2):
        a_step(h, 6)
    wait_blocks(2)
    lax.fori_loop(0, TILES, third_group, 0)
    for h in range(2):
        a_step(h, 7)
    wait_blocks(3)
    hear(3)
    lax.fori_loop(0, TILES, last_first, 0)
    send_sums(0)
    lax.fori_loop(0, TILES, last_second, 0)
    send_sums(1)
    take_sums(0)
    take_sums(1)

    book = i * SHARE + s
    lower = jnp.full((PIVOTS, 128), low[book], jnp.int32).astype(F32) * 0.125
    upper = jnp.full((PIVOTS, 128), high[book], jnp.int32).astype(F32) * 0.125
    wanted = jnp.full((PIVOTS, 128), rank[book], jnp.int32).astype(F32)
    levels = lax.broadcasted_iota(jnp.int32, (PIVOTS, 128), 0).astype(F32)
    for h in range(2):
        drain(DV.at[h, pl.ds(0, N_SCEN - 1)], d_recv.at[h])
    share_sums(0)
    share_sums(1)
    for _ in range(ROUNDS):
        spacing = (upper - lower) / (PIVOTS - 1)
        marks = lower + levels * spacing
        count = jnp.zeros((PIVOTS, 128), F32)
        for h in range(2):
            for p in range(N_SCEN):
                for r in range(2):
                    row = DV[h, p, pl.ds(r, 1), :]
                    count = count + jnp.where(row <= marks, 1.0, 0.0)
        count = jnp.sum(count, axis=1, keepdims=True)
        below = jnp.sum(jnp.where(count < wanted, 1.0, 0.0), axis=0, keepdims=True)
        chosen = jnp.clip(below, 1.0, PIVOTS - 1.0)
        upper = lower + chosen * spacing
        lower = lower + (chosen - 1.0) * spacing
    quantile = (lower + upper) * 0.5
    pair_q = quantile[0:2, :]
    mass = jnp.zeros((2, 128), F32)
    for h in range(2):
        for p in range(N_SCEN):
            mass = mass + sigmoid((pair_q - DV[h, p]) * 2.0).astype(BF16).astype(F32)
    mass = jnp.sum(jnp.sum(mass, axis=1, keepdims=True), axis=0, keepdims=True)
    lane = lax.broadcasted_iota(jnp.int32, (1, 128), 1)
    QR[s] = jnp.where(lane < 64, quantile[0:1, :], jnp.broadcast_to(mass, (1, 128)))

    for p in scen_peers():
        remote(QR.at[s], QR.at[s], f_send.at[0], f_recv.at[0], scen=p).start()
    drain(QR.at[pl.ds(0, N_SCEN - 1)], f_recv.at[0])

    line = lax.broadcasted_iota(jnp.int32, (SHARE, 128), 0)
    lane = lax.broadcasted_iota(jnp.int32, (SHARE, 128), 1)
    at_q, at_mass = lane == line, lane == line + 64
    row_q = jnp.sum(jnp.where(at_q | at_mass, QR[:, 0, :], 0.0), axis=0, keepdims=True)
    QA[i] = row_q
    for p in inst_peers():
        remote(QA.at[i], QA.at[i], f_send.at[1], f_recv.at[1], inst=p).start()
    qout[...] = row_q[0, :SHARE]

    def column(t, where):
        return jnp.sum(jnp.where(where, jnp.broadcast_to(QA[t], (SHARE, 128)), 0.0), axis=1, keepdims=True)

    for h in range(2):
        drain(PNL.at[pl.ds(0, N_INST - 1), h], g_recv.at[h])
    drain(QA.at[pl.ds(0, N_INST - 1)], f_recv.at[1])

    for t in range(N_INST):
        ahead = lax.rem(t // 2 - z + RING, RING)
        order = jnp.where(ahead == 0, 7, jnp.where(ahead < 4, 7 - 2 * ahead, 2 * ahead - 8))
        place = jnp.where(c == t % 2, BOOKS // 2, 0) + order * SHARE
        q = column(t, at_q)
        for h in range(2):
            w = sigmoid((q - PNL[t, h]) * 2.0).astype(BF16)
            W[pl.ds(pl.multiple_of(place, SHARE), SHARE), pl.ds(h * HALF, HALF)] = w

    own_mass = column(s, at_mass)

    def chunk_cols(n):
        return pl.ds(n * CHUNK, CHUNK)

    def sib_copy(k):
        if k < CHUNKS:
            part = (pl.ds(0, SHARE), chunk_cols(k))
        elif k < 2 * CHUNKS:
            part = (pl.ds(SHARE, 2 * SHARE), chunk_cols(k - CHUNKS))
        else:
            start, size = ((3, 2), (5, 3))[k - 2 * CHUNKS]
            part = (pl.ds(start * SHARE, size * SHARE), pl.ds(0, INST_DEV))
        return remote(SIBS.at[part], SIBR.at[part], sib_send.at[k], sib_recv.at[k], scen=partner)

    def contribute(n):
        for u in range(2):
            cols = pl.ds(n * CHUNK + u * (CHUNK // 2), CHUNK // 2)
            both = jnp.dot(W[...], PR[:, cols], preferred_element_type=F32)
            SIBS[:, cols] = both[: BOOKS // 2].astype(BF16)
            OWNC[:, cols] = both[BOOKS // 2 :]
        sib_copy(n).start()
        sib_copy(CHUNKS + n).start()

    def ring_copy(n, way, step):
        if step == 0:
            cols = pl.ds(way * (CHUNK // 2), CHUNK // 2)
        else:
            cols = pl.ds(0, CHUNK)
        slot = (n * 2 + way) * 4 + step
        return remote(
            RSND.at[slot, :, cols], RRCV.at[slot, :, cols], r_send.at[slot], r_recv.at[slot],
            scen=up if way == 0 else down,
        )

    def held(n, step, way, u, count):
        order = 0 if step == 0 else 7 if step == 4 else 2 * step - 1 + way
        rows = pl.ds(order * SHARE, SHARE)
        cols = pl.ds(n * CHUNK + u * (CHUNK // 2), count * (CHUNK // 2))
        return OWNC[rows, cols] + SIBR[rows, cols].astype(F32)

    def ring_step(n, step):
        halves = (pl.ds(0, CHUNK // 2), pl.ds(CHUNK // 2, CHUNK // 2))
        if step == 4:
            ring_copy(n, 0, 3).wait_recv()
            ring_copy(n, 1, 3).wait_recv()
            total = held(n, 4, 0, 0, 2)
            total = total + RRCV[(n * 2) * 4 + 3].astype(F32) + RRCV[(n * 2 + 1) * 4 + 3].astype(F32)
            out[:, chunk_cols(n)] = total / own_mass
            return
        for way in range(2):
            slot = (n * 2 + way) * 4 + step
            if step == 0:
                RSND[slot, :, halves[way]] = held(n, 0, way, way, 1).astype(BF16)
            else:
                ring_copy(n, way, step - 1).wait_recv()
                for u in range(2):
                    v = held(n, step, way, u, 1)
                    if step > 1 or u == way:
                        v = v + RRCV[slot - 1, :, halves[u]].astype(F32)
                    RSND[slot, :, halves[u]] = v.astype(BF16)
            ring_copy(n, way, step).start()

    def first_step(n):
        sib_copy(n).wait_recv()
        ring_step(n, 0)

    for n in range(CHUNKS):
        contribute(n)
    for k in range(2):
        sib_copy(2 * CHUNKS + k).start()
    for n in range(CHUNKS):
        first_step(n)
    for n in range(CHUNKS):
        sib_copy(CHUNKS + n).wait_recv()
        ring_step(n, 1)
    sib_copy(2 * CHUNKS).wait_recv()
    for n in range(CHUNKS):
        ring_step(n, 2)
    sib_copy(2 * CHUNKS + 1).wait_recv()
    for n in range(CHUNKS):
        ring_step(n, 3)
    for n in range(CHUNKS):
        ring_step(n, 4)

    drain(LH.at[pl.ds(0, N_INST - 1)], a_send)
    for h in range(2):
        drain(RS.at[h, pl.ds(0, N_INST - 1)], c_send.at[h])
        drain(DV.at[h, pl.ds(0, N_SCEN - 1)], d_send.at[h])
        drain(PNL.at[pl.ds(0, N_INST - 1), h], g_send.at[h])
    drain(QR.at[pl.ds(0, N_SCEN - 1)], f_send.at[0])
    drain(QA.at[pl.ds(0, N_INST - 1)], f_send.at[1])
    for k in range(2 * CHUNKS + 2):
        sib_copy(k).wait_send()
    for n in range(CHUNKS):
        for way in range(2):
            for step in range(4):
                ring_copy(n, way, step).wait_send()


def body(shocks, loadings, delta, gamma, kappa, book_of, bracket_low, bracket_high, rank):
    anywhere = pl.BlockSpec(memory_space=pl.ANY)
    row = lambda v: v.reshape(1, INST_DEV)
    dma = pltpu.SemaphoreType.DMA
    out, q = pl.pallas_call(
        kernel,
        out_shape=(
            pltpu.VMEM((SHARE, INST_DEV), F32),
            pltpu.VMEM((SHARE,), F32),
        ),
        in_specs=[anywhere] * 9,
        out_specs=(pl.BlockSpec(memory_space=pltpu.VMEM),) * 2,
        scratch_shapes=[
            pltpu.SMEM((BOOKS,), jnp.int32),
            pltpu.SMEM((BOOKS,), jnp.int32),
            pltpu.SMEM((BOOKS,), jnp.int32),
            pltpu.VMEM((N_INST, SCEN_DEV, FACT_DEV), BF16),
            pltpu.VMEM((FACTORS, INST_DEV), BF16),
            pltpu.VMEM((SCEN_DEV, INST_DEV), F32),
            pltpu.VMEM((SCEN_DEV, INST_DEV), BF16),
            pltpu.VMEM((INST_DEV, BOOKS), BF16),
            pltpu.VMEM((3, 1, INST_DEV), F32),
            pltpu.VMEM((1, INST_DEV), jnp.int32),
            pltpu.VMEM((2, HALF, BOOKS), F32),
            pltpu.VMEM((2, BOOKS, HALF), F32),
            pltpu.VMEM((2, N_INST, SHARE, HALF), F32),
            pltpu.VMEM((2, SHARE, 2, 128), F32),
            pltpu.VMEM((2, N_SCEN, 2, 128), F32),
            pltpu.VMEM((N_INST, 2, SHARE, HALF), F32),
            pltpu.VMEM((SHARE, 1, 128), F32),
            pltpu.VMEM((N_INST, 1, 128), F32),
            pltpu.VMEM((BOOKS, SCEN_DEV), BF16),
            pltpu.VMEM((BOOKS // 2, INST_DEV), BF16),
            pltpu.VMEM((BOOKS // 2, INST_DEV), BF16),
            pltpu.VMEM((BOOKS // 2, INST_DEV), F32),
            pltpu.VMEM((CHUNKS * 8, SHARE, CHUNK), BF16),
            pltpu.VMEM((CHUNKS * 8, SHARE, CHUNK), BF16),
            pltpu.SemaphoreType.REGULAR((4,)),
            dma((N_INST,)),
            dma((8,)),
            dma(()),
            dma((80,)),
            dma((2,)), dma((2,)),
            dma((2,)), dma((2,)),
            dma((2,)), dma((2,)),
            dma((2,)), dma((2,)),
            dma((2 * CHUNKS + 2,)), dma((2 * CHUNKS + 2,)),
            dma((CHUNKS * 8,)), dma((CHUNKS * 8,)),
        ],
        compiler_params=pltpu.CompilerParams(
            collective_id=0, has_side_effects=True, vmem_limit_bytes=60 * 1024 * 1024
        ),
        name="revalue",
    )(
        shocks, loadings, row(delta), row(gamma), row(kappa), row(book_of),
        bracket_low, bracket_high, rank,
    )
    return out, q


def solution(mesh):
    placed = (
        P("scen", "inst"),
        P(None, "inst"),
        P("inst"),
        P("inst"),
        P("inst"),
        P("inst"),
        P(),
        P(),
        P(),
    )
    return jax.shard_map(
        body, mesh=mesh, in_specs=placed, out_specs=(P("scen", "inst"), P("inst")), check_vma=False
    )
```
